32 devices in a mesh: dp: 8 (over y, x, core), tensor: 4 (over z).
Axes of the slice: x: 2, y: 2, z: 4, core: 2. Of those that a mesh axis runs over, the one named last changes fastest.
Arguments:
- tokens: bfloat16 [4096, 1024], P(('dp', 'tensor')), may hold values from -6 to 6
- seg_ids: int32 [8, 512], P('dp'), may hold values from 0 to 3, never falling along the last dimension, each value on 1 to 256 neighbouring positions
- attn_gain: float32 [1024], replicated, may hold values from 0.5 to 1.5
- w_query: bfloat16 [1024, 1024], P(None, 'tensor'), may hold values from -0.1875 to 0.1875
- w_key: bfloat16 [1024, 1024], P(None, 'tensor'), may hold values from -0.1875 to 0.1875
- w_value: bfloat16 [1024, 2048], P(None, 'tensor'), may hold values from -0.1875 to 0.1875
- w_gate: bfloat16 [1024, 2048], P(None, 'tensor'), may hold values from -0.1875 to 0.1875
- w_decay: bfloat16 [1024, 8], P(None, 'tensor'), may hold values from -0.1875 to 0.1875
- w_beta: bfloat16 [1024, 8], P(None, 'tensor'), may hold values from -0.1875 to 0.1875
- conv_query: float32 [4, 1024], P(None, 'tensor'), may hold values from -3 to 3
- conv_key: float32 [4, 1024], P(None, 'tensor'), may hold values from -3 to 3
- conv_value: float32 [4, 2048], P(None, 'tensor'), may hold values from -3 to 3
- decay_rate: float32 [8], P('tensor'), may hold values from 0.005 to 1
- out_gain: float32 [256], replicated, may hold values from 0.5 to 1.5
- w_out: bfloat16 [2048, 1024], P('tensor'), may hold values from -0.25 to 0.25
- ffn_gain: float32 [1024], replicated, may hold values from 0.5 to 1.5
- w_ffn_gate: bfloat16 [1024, 2816], P(None, 'tensor'), may hold values from -0.1875 to 0.1875
- w_ffn_up: bfloat16 [1024, 2816], P(None, 'tensor'), may hold values from -0.1875 to 0.1875
- w_ffn_down: bfloat16 [2816, 1024], P('tensor'), may hold values from -0.21875 to 0.21875
- grad_out: bfloat16 [4096, 1024], P(('dp', 'tensor')), may hold values from -6 to 6
Outputs:
- block_out: bfloat16 [4096, 1024], P(('dp', 'tensor'))
- grad_tokens: bfloat16 [4096, 1024], P(('dp', 'tensor'))
- grad_attn_gain: float32 [1024], replicated
- grad_w_query: float32 [1024, 1024], P('dp', 'tensor')
- grad_w_key: float32 [1024, 1024], P('dp', 'tensor')
- grad_w_value: float32 [1024, 2048], P('dp', 'tensor')
- grad_w_gate: float32 [1024, 2048], P('dp', 'tensor')
- grad_w_decay: float32 [1024, 8], P('dp', 'tensor')
- grad_w_beta: float32 [1024, 8], P('dp', 'tensor')
- grad_conv_query: float32 [4, 1024], P(None, 'tensor')
- grad_conv_key: float32 [4, 1024], P(None, 'tensor')
- grad_conv_value: float32 [4, 2048], P(None, 'tensor')
- grad_decay_rate: float32 [8], P('tensor')
- grad_out_gain: float32 [256], replicated
- grad_w_out: float32 [2048, 1024], P('tensor', 'dp')
- grad_ffn_gain: float32 [1024], replicated
- grad_w_ffn_gate: float32 [1024, 2816], P('dp', 'tensor')
- grad_w_ffn_up: float32 [1024, 2816], P('dp', 'tensor')
- grad_w_ffn_down: float32 [2816, 1024], P('tensor', 'dp')
The draws below stay inside these ranges and needn't reach their ends.
Inputs may be any that keep to these rules, and one draw needn't show every extreme that they name: `seg_ids`: along each sequence the document numbers never fall; each document has 1 to 256 tokens.
All inputs are finite; a program needn't handle non-finite values.
Results may differ from the reference program's by a relative error of at most 0.018.
Values may be sent and summed in bfloat16 or wider, within the bound.
A program may use at most 192 MiB of HBM per device.

```python
import math
from functools import partial
import jax
import jax.numpy as jnp
import numpy as np
from jax import lax

D = 1024
HEADS = 8
KEY_DIM = 128
VAL_DIM = 256
FF = 2816
CONV = 4
GROUP = 64
LEN = 512
SEQS = 8
TOKENS = 4096


def steps_of(stream_key, extent, pieces, low, largest):
    def one(dim, blocks):
        heights = jax.random.uniform(jax.random.fold_in(jax.random.fold_in(stream_key, 6), dim), (blocks,), jnp.float32, low / len(pieces), largest / len(pieces))
        return jnp.repeat(jnp.exp(heights), extent[dim] // blocks).reshape((-1,) + (1,) * (len(extent) - dim - 1))

    level = one(*pieces[0])
    for cut in pieces[1:]:
        level = level * one(*cut)
    return level


def split_up(amount, total, reach, slope):
    weights = [(1 << 20) // math.isqrt(grade ** slope) + 1 for grade in range(2, amount + 1)]
    spare, holding = total - reach - (amount - 1), [1] * (amount - 1)
    while spare > 0:
        candidates = [i for i in range(amount - 1) if holding[i] < reach]
        whole, budget = sum([weights[i] for i in candidates]), spare
        for i in candidates:
            more = min(reach - holding[i], max(1, budget * weights[i] // whole), spare)
            holding[i] = holding[i] + more
            spare = spare - more
    return np.array([reach] + holding)


def uneven_parts(own_key, number_of, total, bound, lean):
    if number_of == 2:
        one = jax.random.randint(own_key, (), max(1, total - bound), min(bound, total - 1) + 1)
        return jnp.stack([one, total - one])
    sizes = jnp.asarray(split_up(number_of, total, bound, lean), jnp.int32)
    pairs = (number_of - 1) // 2
    donor, taker = sizes[1:1 + 2 * pairs:2], sizes[2:2 + 2 * pairs:2]
    room = jnp.minimum(donor - 1, bound - taker)
    shifted = jax.random.randint(jax.random.fold_in(own_key, 1), (pairs,), 0, 1 << 20) % (room + 1)
    sizes = sizes.at[1:1 + 2 * pairs:2].set(donor - shifted).at[2:2 + 2 * pairs:2].set(taker + shifted)
    return sizes[jax.random.permutation(jax.random.fold_in(own_key, 2), number_of)]


def gaussian(stream_key, dims, scale, bound, cuts=(), held_as=jnp.bfloat16):
    drawn = jax.random.normal(stream_key, dims, jnp.float32) * scale
    if len(cuts) > 0:
        drawn = steps_of(stream_key, dims, cuts, -0.22, 0.18) * drawn
    return jnp.clip(drawn, min=-bound, max=bound).astype(held_as)


def setup_inputs(seed: int = 0) -> dict:
    arg_keys = jax.random.split(jax.random.key(seed), 21)
    return {
        "tokens": gaussian(arg_keys[0], (TOKENS, D), 1.0, 6.0, ((0, 32),)),
        "seg_ids": jax.vmap(lambda own: jnp.searchsorted(jnp.cumsum(uneven_parts(own, 4, LEN, LEN // 2, 1)), jnp.arange(LEN), side="right"))(jax.random.split(arg_keys[1], SEQS)).reshape((SEQS, LEN)).astype(jnp.int32),
        "attn_gain": jnp.clip(1.0 + 0.1 * jax.random.normal(arg_keys[2], (D,), jnp.float32), 0.5, 1.5),
        "w_query": gaussian(arg_keys[3], (D, HEADS * KEY_DIM), D ** -0.5, 0.1875, ((1, 4),)),
        "w_key": gaussian(arg_keys[4], (D, HEADS * KEY_DIM), D ** -0.5, 0.1875, ((1, 4),)),
        "w_value": gaussian(arg_keys[5], (D, HEADS * VAL_DIM), D ** -0.5, 0.1875, ((1, 4),)),
        "w_gate": gaussian(arg_keys[6], (D, HEADS * VAL_DIM), D ** -0.5, 0.1875, ((1, 4),)),
        "w_decay": gaussian(arg_keys[7], (D, HEADS), D ** -0.5, 0.1875, ((1, 4),)),
        "w_beta": gaussian(arg_keys[8], (D, HEADS), D ** -0.5, 0.1875, ((1, 4),)),
        "conv_query": gaussian(arg_keys[9], (CONV, HEADS * KEY_DIM), CONV ** -0.5, 3.0, ((1, 4),), jnp.float32),
        "conv_key": gaussian(arg_keys[10], (CONV, HEADS * KEY_DIM), CONV ** -0.5, 3.0, ((1, 4),), jnp.float32),
        "conv_value": gaussian(arg_keys[11], (CONV, HEADS * VAL_DIM), CONV ** -0.5, 3.0, ((1, 4),), jnp.float32),
        "decay_rate": jnp.clip(jnp.exp(math.log(1.0) - 5.2983174 * jax.random.uniform(arg_keys[12], (HEADS,), jnp.float32) ** steps_of(arg_keys[12], (HEADS,), ((0, 4),), -0.2, 0.2)), 0.005, 1.0),
        "out_gain": jnp.clip(1.0 + 0.1 * jax.random.normal(arg_keys[13], (VAL_DIM,), jnp.float32), 0.5, 1.5),
        "w_out": gaussian(arg_keys[14], (HEADS * VAL_DIM, D), (HEADS * VAL_DIM // 4) ** -0.5, 0.25, ((0, 4),)),
        "ffn_gain": jnp.clip(1.0 + 0.1 * jax.random.normal(arg_keys[15], (D,), jnp.float32), 0.5, 1.5),
        "w_ffn_gate": gaussian(arg_keys[16], (D, FF), D ** -0.5, 0.1875, ((1, 4),)),
        "w_ffn_up": gaussian(arg_keys[17], (D, FF), D ** -0.5, 0.1875, ((1, 4),)),
        "w_ffn_down": gaussian(arg_keys[18], (FF, D), (FF // 4) ** -0.5, 0.21875, ((0, 4),)),
        "grad_out": gaussian(arg_keys[19], (TOKENS, D), 1.0, 6.0, ((0, 32),)),
    }


EPS_NORM = 1e-05
EPS_UNIT = 1e-06
HIGH = lax.Precision.HIGHEST

def norm_gain(values, gain):
    return values * lax.rsqrt(lax.optimization_barrier(jnp.mean(values * values, axis=-1, keepdims=True)) + EPS_NORM) * gain

def shift_rows(values, offset, fill):
    padding = jnp.full((offset,) + values.shape[1:], fill, values.dtype)
    return jnp.concatenate([padding, values[:-offset]], axis=0)

def short_conv(values, taps, seg_row):
    total = taps[0] * values
    for offset in range(1, taps.shape[0]):
        keep = (seg_row == shift_rows(seg_row, offset, -1)).astype(values.dtype)
        total = total + taps[offset] * shift_rows(values, offset, 0) * keep[:, None]
    return total

def unit_rows(values):
    return values * lax.rsqrt(lax.optimization_barrier(jnp.sum(values * values, axis=-1, keepdims=True)) + EPS_UNIT)

def delta_block(carry, block):
    state, prev_doc = carry
    query, keys, values, beta, log_decay, doc = block
    size = doc.shape[0]
    index = jnp.arange(size)
    lower = index[:, None] >= index[None, :]
    strict = (index[:, None] > index[None, :]).astype(state.dtype)
    same_doc = ((doc[:, None] == doc[None, :]) & lower).astype(state.dtype)
    cum_log = jnp.cumsum(log_decay, axis=0).T
    spread = jnp.exp(jnp.minimum(cum_log[:, :, None] - cum_log[:, None, :], 0.0)) * same_doc[None]
    carried_keep = jnp.exp(cum_log) * (doc == prev_doc).astype(state.dtype)[None, :]
    key_key = jnp.einsum('thd,ihd->hti', keys, keys, precision=HIGH)
    beta_rows = beta.T[:, :, None]
    system = jnp.eye(size, dtype=state.dtype)[None] + beta_rows * key_key * spread * strict[None]
    from_state = jnp.einsum('thd,hde->hte', keys, state, precision=HIGH)
    right_side = beta_rows * (jnp.transpose(values, (1, 0, 2)) - carried_keep[:, :, None] * from_state)
    delta = lax.linalg.triangular_solve(system, right_side, left_side=True, lower=True, unit_diagonal=True)
    query_key = jnp.einsum('thd,ihd->hti', query, keys, precision=HIGH)
    mixed = jnp.einsum('hti,hie->the', query_key * spread, delta, precision=HIGH)
    mixed = mixed + jnp.einsum('thd,hde->the', query * carried_keep.T[:, :, None], state, precision=HIGH)
    final_row = spread[:, -1, :]
    new_state = carried_keep[:, -1][:, None, None] * state + jnp.einsum('ihd,hi,hie->hde', keys, final_row, delta, precision=HIGH)
    return ((new_state, doc[-1]), mixed)

def mixer(seg_row, q_proj, k_proj, v_proj, gate_proj, decay_proj, beta_proj, conv_query, conv_key, conv_value, decay_rate, out_gain):
    length = q_proj.shape[0]
    heads = decay_proj.shape[1]
    key_dim = q_proj.shape[1] // heads
    val_dim = v_proj.shape[1] // heads
    query = unit_rows(jax.nn.silu(short_conv(q_proj, conv_query, seg_row)).reshape(length, heads, key_dim)) / math.sqrt(key_dim)
    keys = unit_rows(jax.nn.silu(short_conv(k_proj, conv_key, seg_row)).reshape(length, heads, key_dim))
    values = jax.nn.silu(short_conv(v_proj, conv_value, seg_row)).reshape(length, heads, val_dim)
    beta = jax.nn.sigmoid(beta_proj)
    log_decay = -decay_rate[None, :] * jax.nn.softplus(decay_proj)
    blocks = length // GROUP

    def split(array):
        return array.reshape((blocks, GROUP) + array.shape[1:])
    init = (jnp.zeros((heads, key_dim, val_dim), q_proj.dtype), jnp.array(-1, dtype=seg_row.dtype))
    _, mixed = lax.scan(delta_block, init, (split(query), split(keys), split(values), split(beta), split(log_decay), split(seg_row)))
    mixed = mixed.reshape(length, heads, val_dim)
    gate = gate_proj.reshape(length, heads, val_dim)
    normed = mixed * lax.rsqrt(lax.optimization_barrier(jnp.mean(mixed * mixed, axis=-1, keepdims=True)) + EPS_NORM) * out_gain * jax.nn.silu(gate)
    return normed.reshape(length, heads * val_dim)

def reference(tokens, seg_ids, attn_gain, w_query, w_key, w_value, w_gate, w_decay, w_beta, conv_query, conv_key, conv_value, decay_rate, out_gain, w_out, ffn_gain, w_ffn_gate, w_ffn_up, w_ffn_down, grad_out):
    seq_count = seg_ids.shape[0]
    length = seg_ids.shape[1]
    width = tokens.shape[1]
    token_seqs = tokens.reshape(seq_count, length, width)
    grad_seqs = grad_out.reshape(seq_count, length, width)
    mats = (w_query, w_key, w_value, w_gate, w_decay, w_beta)
    params = (conv_query, conv_key, conv_value, decay_rate, out_gain)

    def one_seq(carry, item):
        x_seq, dy_seq, seg_row = item
        x_float = x_seq.astype(jnp.float32)
        xnorm = norm_gain(x_float, attn_gain).astype(jnp.bfloat16)
        projs = [jnp.dot(xnorm.astype(jnp.float32), weight.astype(jnp.float32), preferred_element_type=jnp.float32) for weight in mats]
        mixed, pull_mix = jax.vjp(partial(mixer, seg_row), projs[0], projs[1], projs[2], projs[3], projs[4], projs[5], params[0], params[1], params[2], params[3], params[4])
        gated = mixed.astype(jnp.bfloat16)
        resid = x_float + jnp.dot(gated.astype(jnp.float32), w_out.astype(jnp.float32), preferred_element_type=jnp.float32)
        hnorm = norm_gain(resid, ffn_gain).astype(jnp.bfloat16)
        up_in = jnp.dot(hnorm.astype(jnp.float32), w_ffn_gate.astype(jnp.float32), preferred_element_type=jnp.float32)
        up_val = jnp.dot(hnorm.astype(jnp.float32), w_ffn_up.astype(jnp.float32), preferred_element_type=jnp.float32)
        act = (jax.nn.silu(up_in) * up_val).astype(jnp.bfloat16)
        out_seq = (resid + jnp.dot(act.astype(jnp.float32), w_ffn_down.astype(jnp.float32), preferred_element_type=jnp.float32)).astype(jnp.bfloat16)
        d_act = jnp.dot(dy_seq.astype(jnp.float32), w_ffn_down.T.astype(jnp.float32), preferred_element_type=jnp.float32)
        g_down = jnp.dot(act.T.astype(jnp.float32), dy_seq.astype(jnp.float32), preferred_element_type=jnp.float32)
        gate_sig = jax.nn.sigmoid(up_in)
        d_up_in = (d_act * up_val * gate_sig * (1.0 + up_in * (1.0 - gate_sig))).astype(jnp.bfloat16)
        d_up_val = (d_act * up_in * gate_sig).astype(jnp.bfloat16)
        g_fgate = jnp.dot(hnorm.T.astype(jnp.float32), d_up_in.astype(jnp.float32), preferred_element_type=jnp.float32)
        g_fup = jnp.dot(hnorm.T.astype(jnp.float32), d_up_val.astype(jnp.float32), preferred_element_type=jnp.float32)
        d_hnorm = jnp.dot(d_up_in.astype(jnp.float32), w_ffn_gate.T.astype(jnp.float32), preferred_element_type=jnp.float32) + jnp.dot(d_up_val.astype(jnp.float32), w_ffn_up.T.astype(jnp.float32), preferred_element_type=jnp.float32)
        _, pull_mid = jax.vjp(norm_gain, resid, ffn_gain)
        d_resid_norm, g_fgain = pull_mid(d_hnorm)
        d_resid = dy_seq.astype(jnp.float32) + d_resid_norm
        d_resid_b = d_resid.astype(jnp.bfloat16)
        g_out = jnp.dot(gated.T.astype(jnp.float32), d_resid_b.astype(jnp.float32), preferred_element_type=jnp.float32)
        d_gated = jnp.dot(d_resid_b.astype(jnp.float32), w_out.T.astype(jnp.float32), preferred_element_type=jnp.float32)
        back = pull_mix(d_gated)
        d_projs = [grad.astype(jnp.bfloat16) for grad in back[:6]]
        g_mats = [jnp.dot(xnorm.T.astype(jnp.float32), grad.astype(jnp.float32), preferred_element_type=jnp.float32) for grad in d_projs]
        d_xnorm = jnp.dot(d_projs[0].astype(jnp.float32), mats[0].T.astype(jnp.float32), preferred_element_type=jnp.float32)
        for grad, weight in zip(d_projs[1:], mats[1:]):
            d_xnorm = d_xnorm + jnp.dot(grad.astype(jnp.float32), weight.T.astype(jnp.float32), preferred_element_type=jnp.float32)
        _, pull_first = jax.vjp(norm_gain, x_float, attn_gain)
        d_x_norm, g_again = pull_first(d_xnorm)
        dx_seq = (d_resid + d_x_norm).astype(jnp.bfloat16)
        grads = (g_again,) + tuple(g_mats) + tuple(back[6:10]) + (back[10], g_out, g_fgain, g_fgate, g_fup, g_down)
        carry = tuple((total + grad for total, grad in zip(carry, grads)))
        return (carry, (out_seq, dx_seq))
    shapes = (attn_gain,) + mats + params[:4] + (out_gain, w_out, ffn_gain, w_ffn_gate, w_ffn_up, w_ffn_down)
    init = tuple((jnp.zeros(array.shape, jnp.float32) for array in shapes))
    sums, (out_seqs, dx_seqs) = lax.scan(one_seq, init, (token_seqs, grad_seqs, seg_ids))
    block_out = out_seqs.reshape(seq_count * length, width)
    grad_tokens = dx_seqs.reshape(seq_count * length, width)
    return (block_out, grad_tokens, sums[0], sums[1], sums[2], sums[3], sums[4], sums[5], sums[6], sums[7], sums[8], sums[9], sums[10], sums[11], sums[12], sums[13], sums[14], sums[15], sums[16])
```

```python
from functools import partial
import math

import jax
import jax.numpy as jnp
from jax import lax
from jax.experimental import pallas as pl
from jax.experimental.pallas import tpu as pltpu
from jax.sharding import PartitionSpec as P

GROUP = 64
LANES = 128
EPS_NORM = 1e-05
EPS_UNIT = 1e-06
HIGHEST = lax.Precision.HIGHEST
HIGH = lax.Precision.HIGH
F32 = jnp.float32
BF16 = jnp.bfloat16
MESH = pl.DeviceIdType.MESH
NN = (((1,), (0,)), ((), ()))
NT = (((1,), (1,)), ((), ()))
TN = (((0,), (0,)), ((), ()))
VMEM_BYTES = 56 << 20


def dot(a, b, dims=NN):
    return lax.dot_general(a.astype(BF16), b.astype(BF16), dims, preferred_element_type=F32)


def dot_fine(a, b, dims=NN):
    return lax.dot_general(a, b, dims, precision=HIGH, preferred_element_type=F32)


def shift_down(values, offset, keep):
    return pltpu.roll(values, offset, 0) * keep


def shift_up(values, offset, keep):
    rolled = values * keep
    return pltpu.roll(rolled, values.shape[0] - offset, 0)


def conv_keeps(seg_col, taps):
    length = seg_col.shape[0]
    row = lax.broadcasted_iota(jnp.int32, (length, LANES), 0)
    seg = jnp.broadcast_to(seg_col, (length, LANES))
    keeps = []
    for offset in range(1, taps):
        same = (seg == pltpu.roll(seg, offset, 0)) & (row >= offset)
        keeps.append(same.astype(F32))
    return keeps


def wide(keep, columns):
    return jnp.concatenate([keep] * (columns // LANES), axis=1) if columns > LANES else keep


def conv(values, taps, keeps):
    total = taps[0:1] * values
    for offset in range(1, taps.shape[0]):
        total = total + taps[offset : offset + 1] * shift_down(
            values, offset, wide(keeps[offset - 1], values.shape[1])
        )
    return total


def conv_back(values, taps, keeps, d_out):
    d_values = taps[0:1] * d_out
    d_taps = [jnp.sum(values * d_out, axis=0, keepdims=True)]
    for offset in range(1, taps.shape[0]):
        keep = wide(keeps[offset - 1], values.shape[1])
        moved = shift_up(d_out, offset, keep)
        d_values = d_values + taps[offset : offset + 1] * moved
        d_taps.append(jnp.sum(values * moved, axis=0, keepdims=True))
    return d_values, jnp.concatenate(d_taps, axis=0)


def softplus(values):
    return jnp.maximum(values, 0.0) + jnp.log1p(jnp.exp(-jnp.abs(values)))


def sigmoid(values):
    return jax.nn.sigmoid(values)


def silu_back(values):
    sig = sigmoid(values)
    return sig * (1.0 + values * (1.0 - sig))


def block_cumsum(values):
    length = values.shape[0]
    row = lax.broadcasted_iota(jnp.int32, values.shape, 0) % GROUP
    step = 1
    while step < GROUP:
        values = values + jnp.where(row >= step, pltpu.roll(values, step, 0), 0.0)
        step *= 2
    return values


def block_cumsum_back(values):
    length = values.shape[0]
    row = lax.broadcasted_iota(jnp.int32, values.shape, 0) % GROUP
    step = 1
    while step < GROUP:
        values = values + jnp.where(
            row < GROUP - step, pltpu.roll(values, length - step, 0), 0.0
        )
        step *= 2
    return values


def invert(lowers):
    size = lowers[0].shape[0]
    rows = lax.broadcasted_iota(jnp.int32, (size, size), 0)
    cols = lax.broadcasted_iota(jnp.int32, (size, size), 1)
    eye = (rows == cols).astype(F32)
    pair = (rows // 2 == cols // 2).astype(F32)
    done = [eye - low * pair for low in lowers]
    half = 2
    while half < size:
        keep = (rows // (2 * half) == cols // (2 * half)) & (rows // half != cols // half)
        keep = keep.astype(F32)
        steps = [dot_fine(low * keep, inv) for low, inv in zip(lowers, done)]
        done = [inv - dot_fine(inv, step) for inv, step in zip(done, steps)]
        half *= 2
    return done


def block_masks(seg_col, seg_row, cum, cum_t, n, h):
    rows = slice(n * GROUP, (n + 1) * GROUP)
    index_t = lax.broadcasted_iota(jnp.int32, (GROUP, GROUP), 0)
    index_i = lax.broadcasted_iota(jnp.int32, (GROUP, GROUP), 1)
    doc_col = seg_col[rows]
    doc_row = seg_row[:, rows]
    c_col = cum[rows, h : h + 1]
    c_row = cum_t[h : h + 1, rows]
    c_last = c_col[GROUP - 1 : GROUP]
    same = ((doc_col == doc_row) & (index_t >= index_i)).astype(F32)
    spread = jnp.exp(jnp.minimum(c_col - c_row, 0.0)) * same
    strict = (index_t > index_i).astype(F32)
    end_doc = doc_col[GROUP - 1 : GROUP]
    late = jnp.exp(jnp.minimum(c_last - c_col, 0.0)) * (doc_col == end_doc).astype(F32)
    if n == 0:
        carried = jnp.zeros_like(c_col)
    else:
        prev = seg_col[n * GROUP - 1 : n * GROUP]
        carried = jnp.exp(c_col) * (doc_col == prev).astype(F32)
    return spread, strict, late, carried


def unit(values):
    rate = lax.rsqrt(jnp.sum(values * values, axis=-1, keepdims=True) + EPS_UNIT)
    return values * rate, rate


def mixer_forward_kernel(
    heads, dk, dv,
    q_ref, k_ref, v_ref, gate_ref, db_ref, seg_col_ref, seg_row_ref,
    tq_ref, tk_ref, tv_ref, rate_ref, ogain_ref,
    gated_ref, inv_ref, delta_ref, state_ref, mixed_ref,
    query, keys, values, carry,
):
    length = q_ref.shape[0]
    blocks = length // GROUP
    seg_col = seg_col_ref[...]
    seg_row = seg_row_ref[...]
    keeps = conv_keeps(seg_col, tq_ref.shape[0])
    db = db_ref[...]
    beta = sigmoid(db)
    cum = block_cumsum(-rate_ref[...] * softplus(db))
    cum_t = cum.T
    scale = 1.0 / math.sqrt(dk)
    for h in range(heads):
        cols = slice(h * dk, (h + 1) * dk)
        query[:, cols] = unit(jax.nn.silu(conv(q_ref[:, cols], tq_ref[:, cols], keeps)))[0] * scale
        keys[:, cols] = unit(jax.nn.silu(conv(k_ref[:, cols], tk_ref[:, cols], keeps)))[0]
        cols = slice(h * dv, (h + 1) * dv)
        values[:, cols] = jax.nn.silu(conv(v_ref[:, cols], tv_ref[:, cols], keeps))

    lowers = []
    for n in range(blocks):
        rows = slice(n * GROUP, (n + 1) * GROUP)
        for h in range(heads):
            key = keys[rows, h * dk : (h + 1) * dk]
            spread, strict, late, carried = block_masks(seg_col, seg_row, cum, cum_t, n, h)
            b = beta[rows, heads + h : heads + h + 1]
            lowers.append(b * dot_fine(key, key, NT) * spread * strict)
    for i, inv in enumerate(invert(lowers)):
        inv_ref[i] = inv

    for h in range(heads):
        carry[h] = jnp.zeros((dk, dv), F32)
    for n in range(blocks):
        rows = slice(n * GROUP, (n + 1) * GROUP)
        for h in range(heads):
            pair = n * heads + h
            kc, vc = slice(h * dk, (h + 1) * dk), slice(h * dv, (h + 1) * dv)
            key, q, v = keys[rows, kc], query[rows, kc], values[rows, vc]
            spread, strict, late, carried = block_masks(seg_col, seg_row, cum, cum_t, n, h)
            b = beta[rows, heads + h : heads + h + 1]
            inv = inv_ref[pair]
            fresh = dot(inv, b * v)
            state = carry[h]
            state_ref[pair] = state
            if n == 0:
                delta = fresh
            else:
                delta = fresh - dot(dot(inv, (b * carried) * key), state)
            delta_ref[rows, vc] = delta
            mixed = dot(dot(q, key, NT) * spread, delta)
            if n > 0:
                mixed = mixed + dot(q * carried, state)
            mixed_ref[rows, vc] = mixed
            if n < blocks - 1:
                new = dot(key * late, delta, TN)
                if n > 0:
                    new = new + carried[GROUP - 1 : GROUP] * state
                carry[h] = new
    for h in range(heads):
        vc = slice(h * dv, (h + 1) * dv)
        mixed = mixed_ref[:, vc]
        rate = lax.rsqrt(jnp.mean(mixed * mixed, axis=-1, keepdims=True) + EPS_NORM)
        gated_ref[:, vc] = (mixed * rate * ogain_ref[...] * jax.nn.silu(gate_ref[:, vc])).astype(BF16)


def vmem_specs(count):
    return [pl.BlockSpec(memory_space=pltpu.VMEM)] * count


def mixer_backward_kernel(
    heads, dk, dv,
    q_ref, k_ref, v_ref, gate_ref, db_ref, seg_col_ref, seg_row_ref,
    tq_ref, tk_ref, tv_ref, rate_ref, ogain_ref,
    inv_ref, delta_ref, state_ref, mixed_ref, dgated_ref,
    d_ref, gq_ref, gk_ref, gv_ref, grate_ref, gogain_ref,
    keys, query, values, d_mixed, d_key, d_query, d_value, d_carry, d_cum, d_beta,
    tick=None,
):
    length = q_ref.shape[0]
    blocks = length // GROUP
    seg_col = seg_col_ref[...]
    seg_row = seg_row_ref[...]
    keeps = conv_keeps(seg_col, tq_ref.shape[0])
    db = db_ref[...]
    beta = sigmoid(db)
    rate_row = rate_ref[...]
    soft = softplus(db)
    cum = block_cumsum(-rate_row * soft)
    cum_t = cum.T
    scale = 1.0 / math.sqrt(dk)
    v_base = 2 * heads * dk
    g_base = v_base + heads * dv
    b_base = g_base + heads * dv

    g_ogain = jnp.zeros((1, dv), F32)
    for h in range(heads):
        vc = slice(h * dv, (h + 1) * dv)
        mixed = mixed_ref[:, vc]
        gate = gate_ref[:, vc]
        dg = dgated_ref[:, vc]
        rate = lax.rsqrt(jnp.mean(mixed * mixed, axis=-1, keepdims=True) + EPS_NORM)
        plain = mixed * rate
        sig = sigmoid(gate)
        d_norm = dg * gate * sig
        d_ref[:, g_base + h * dv : g_base + (h + 1) * dv] = (
            dg * plain * ogain_ref[...] * sig * (1.0 + gate * (1.0 - sig))
        ).astype(BF16)
        g_ogain = g_ogain + jnp.sum(d_norm * plain, axis=0, keepdims=True)
        up = d_norm * ogain_ref[...]
        d_mixed[:, vc] = rate * (up - plain * jnp.mean(up * plain, axis=-1, keepdims=True))
        kc = slice(h * dk, (h + 1) * dk)
        query[:, kc] = unit(jax.nn.silu(conv(q_ref[:, kc], tq_ref[:, kc], keeps)))[0] * scale
        keys[:, kc] = unit(jax.nn.silu(conv(k_ref[:, kc], tk_ref[:, kc], keeps)))[0]
        values[:, vc] = jax.nn.silu(conv(v_ref[:, vc], tv_ref[:, vc], keeps))
        d_carry[h] = jnp.zeros((dk, dv), F32)
    gogain_ref[...] = g_ogain
    tick(1)

    lane = lax.broadcasted_iota(jnp.int32, (GROUP, LANES), 1)
    row_col = lax.broadcasted_iota(jnp.int32, (GROUP, 1), 0)
    index_t = lax.broadcasted_iota(jnp.int32, (GROUP, GROUP), 0)
    index_i = lax.broadcasted_iota(jnp.int32, (GROUP, GROUP), 1)
    eye = (index_t == index_i).astype(F32)
    for n in reversed(range(blocks)):
        rows = slice(n * GROUP, (n + 1) * GROUP)
        dc_block = jnp.zeros((GROUP, LANES), F32)
        db_block = jnp.zeros((GROUP, LANES), F32)
        last = n == blocks - 1
        for h in range(heads):
            pair = n * heads + h
            kc, vc = slice(h * dk, (h + 1) * dk), slice(h * dv, (h + 1) * dv)
            key, q, v = keys[rows, kc], query[rows, kc], values[rows, vc]
            spread, strict, late, a = block_masks(seg_col, seg_row, cum, cum_t, n, h)
            b = beta[rows, heads + h : heads + h + 1]
            inv = inv_ref[pair]
            delta = delta_ref[rows, vc]
            state = state_ref[pair]
            d_out = d_mixed[rows, vc]
            d_next = d_carry[h]
            key_late = key * late
            gram = dot(key, key, NT)
            score = dot(q, key, NT)
            d_score = dot(d_out, delta, NT)
            d_delta = dot(score * spread, d_out, TN)
            if not last:
                d_delta = d_delta + dot(key_late, d_next)
            d_right = dot(inv, d_delta, TN)
            d_lower = -dot(d_right, delta, NT) * strict
            d_value[rows, vc] = b * d_right
            dk_sum = jnp.zeros((GROUP, dk), F32)
            dq_sum = jnp.zeros((GROUP, dk), F32)
            d_b = jnp.sum(d_right * v, axis=-1, keepdims=True)
            d_c = jnp.zeros((GROUP, 1), F32)
            if n > 0:
                d_from = (-b * a) * d_right
                from_state = dot(key, state)
                d_b = d_b - a * jnp.sum(d_right * from_state, axis=-1, keepdims=True)
                dk_sum = dk_sum + dot(d_from, state, NT)
                reads = dot(d_out, state, NT)
                dq_sum = dq_sum + a * reads
                d_a = jnp.sum(q * reads, axis=-1, keepdims=True) - b * jnp.sum(
                    d_right * from_state, axis=-1, keepdims=True
                )
                d_state = dot(q * a, d_out, TN) + dot(key, d_from, TN)
                if not last:
                    a_last = a[GROUP - 1 : GROUP]
                    d_state = d_state + a_last * d_next
                    d_a = d_a + jnp.where(
                        row_col == GROUP - 1,
                        jnp.sum(jnp.sum(state * d_next, axis=-1, keepdims=True), axis=0, keepdims=True),
                        0.0,
                    )
                d_carry[h] = d_state
                d_c = d_c + d_a * a
            if not last:
                d_late_key = dot(delta, d_next, NT)
                dk_sum = dk_sum + late * d_late_key
                d_late = late * jnp.sum(key * d_late_key, axis=-1, keepdims=True)
                d_c = d_c - d_late + jnp.where(
                    row_col == GROUP - 1, jnp.sum(d_late, axis=0, keepdims=True), 0.0
                )
            d_pair = d_score * spread
            dq_sum = dq_sum + dot(d_pair, key)
            dk_sum = dk_sum + dot(d_pair, q, TN)
            gram_spread = gram * spread
            d_b = d_b + jnp.sum(d_lower * gram_spread, axis=-1, keepdims=True)
            d_gram = d_lower * (b * spread)
            dk_sum = dk_sum + dot(d_gram, key) + dot(d_gram, key, TN)
            cross = d_pair * score + d_gram * gram
            d_c = d_c + jnp.sum(cross, axis=-1, keepdims=True)
            falls = jnp.sum(cross, axis=0, keepdims=True)
            d_c = d_c - jnp.sum(eye * falls, axis=-1, keepdims=True)
            d_key[rows, kc] = dk_sum
            d_query[rows, kc] = dq_sum
            dc_block = dc_block + jnp.where(lane == h, d_c, 0.0)
            db_block = db_block + jnp.where(lane == heads + h, d_b, 0.0)
        d_cum[rows, :] = dc_block
        d_beta[rows, :] = db_block

    tick(2)
    d_log = block_cumsum_back(d_cum[...])
    grate_ref[...] = jnp.sum(d_log * -soft, axis=0, keepdims=True)
    sig = beta
    d_ref[:, b_base : b_base + LANES] = (
        d_log * -rate_row * sig + d_beta[...] * sig * (1.0 - sig)
    ).astype(BF16)

    for h in range(heads):
        kc, vc = slice(h * dk, (h + 1) * dk), slice(h * dv, (h + 1) * dv)
        for ref, taps, g_ref, d_unit, base, factor in (
            (q_ref, tq_ref, gq_ref, d_query, 0, scale),
            (k_ref, tk_ref, gk_ref, d_key, heads * dk, 1.0),
        ):
            proj = ref[:, kc]
            pre = conv(proj, taps[:, kc], keeps)
            act = jax.nn.silu(pre)
            normed, rate = unit(act)
            up = d_unit[:, kc] * factor
            d_act = rate * (up - normed * jnp.sum(up * normed, axis=-1, keepdims=True))
            d_proj, d_taps = conv_back(proj, taps[:, kc], keeps, d_act * silu_back(pre))
            d_ref[:, base + h * dk : base + (h + 1) * dk] = d_proj.astype(BF16)
            g_ref[:, kc] = d_taps
        proj = v_ref[:, vc]
        pre = conv(proj, tv_ref[:, vc], keeps)
        d_proj, d_taps = conv_back(proj, tv_ref[:, vc], keeps, d_value[:, vc] * silu_back(pre))
        d_ref[:, v_base + h * dv : v_base + (h + 1) * dv] = d_proj.astype(BF16)
        gv_ref[:, vc] = d_taps


def rows_of(index, count):
    return pl.ds(pl.multiple_of(index * count, count), count)


def enter(targets):
    barrier = pltpu.get_barrier_semaphore()
    for target in targets:
        pl.semaphore_signal(barrier, inc=1, device_id=target, device_id_type=MESH)
    pl.semaphore_wait(barrier, len(targets))


def order_of(n):
    steps = []
    for k in range(1, n // 2 + 1):
        steps.append(k)
        if n - k != k:
            steps.append(n - k)
    return steps


class Ring:
    def __init__(self, n):
        self.n = n
        self.me = lax.axis_index("tensor")
        self.steps = order_of(n)

    def to(self, k):
        return lax.rem(self.me + k, self.n)

    def source(self, k):
        return lax.rem(self.me + self.n - k, self.n)

    def targets(self):
        return [{"tensor": self.to(k)} for k in self.steps]

    def copy(self, k, src, dst, send, recv):
        return pltpu.make_async_remote_copy(
            src_ref=src, dst_ref=dst, send_sem=send.at[k - 1], recv_sem=recv.at[k - 1],
            device_id={"tensor": self.to(k)}, device_id_type=MESH,
        )

    def share(self, ref, send, recv):
        copies = {}
        for k in self.steps:
            copies[k] = self.copy(k, ref.at[self.me], ref.at[self.me], send, recv)
            copies[k].start()
        return copies


class Scatter:
    def __init__(self, bits, source, result, inbox, total, streams, sems):
        self.bits, self.source, self.result = bits, source, result
        self.inbox, self.total, self.streams, self.sems = inbox, total, streams, sems
        self.dp = lax.axis_index("dp")
        self.copies = []

    def bit(self, b):
        return lax.rem(self.dp // (1 << b), 2)

    def partner(self, b):
        return {"dp": self.dp + (1 - 2 * self.bit(b)) * (1 << b)}

    def targets(self):
        return [self.partner(b) for b in range(self.bits)]

    def send(self, b, src, dst, slot):
        copy = pltpu.make_async_remote_copy(
            src_ref=src, dst_ref=dst, send_sem=self.sems.at[0, slot], recv_sem=self.sems.at[1, slot],
            device_id=self.partner(b), device_id_type=MESH,
        )
        copy.start()
        self.copies.append(copy)
        return copy

    def orders(self):
        rest = list(range(1, self.bits))
        return rest, rest[::-1]

    def step(self, phase):
        if phase == 0:
            lead = (slice(None),) * (self.bits - 1)
            self.waiting = [self.send(0, self.source.at[lead + (1 - self.bit(0),)], self.inbox, 0)]
            return
        if phase == 1:
            lead = (slice(None),) * (self.bits - 1)
            self.waiting[0].wait_recv()
            self.total[...] = (
                self.source[lead + (self.bit(0),)].astype(F32) + self.inbox[...].astype(F32)
            ).astype(BF16)
            self.held = [(self.total, list(range(self.bits - 1, 0, -1)))] * 2
        waiting = []
        for s, order in enumerate(self.orders()):
            low, high, sums, boxes = self.streams[s]
            if phase > 1:
                b = order[phase - 2]
                ref, axes = self.held[s]
                self.waiting[s].wait_recv()
                columns = (slice(None), slice(low, high) if phase == 2 else slice(None))
                lead = tuple(self.bit(b) if a == b else slice(None) for a in axes)
                value = ref[lead + columns].astype(F32) + boxes[phase - 2][...].astype(F32)
                if phase == self.bits:
                    self.result[:, low:high] = value
                else:
                    sums[phase - 2][...] = value.astype(BF16)
                    self.held[s] = (sums[phase - 2], [a for a in axes if a != b])
            if phase < self.bits:
                b = order[phase - 1]
                ref, axes = self.held[s]
                columns = (slice(None), slice(low, high) if phase == 1 else slice(None))
                lead = tuple(1 - self.bit(b) if a == b else slice(None) for a in axes)
                slot = 1 + s * (self.bits - 1) + phase - 1
                waiting.append(self.send(b, ref.at[lead + columns], boxes[phase - 1], slot))
        self.waiting = waiting

    def finish(self):
        for copy in self.copies:
            copy.wait_send()


def scatter_scratch(bits, rows, width):
    middle = width // (2 * LANES) * LANES
    shapes = [
        pltpu.VMEM((rows, width), F32),
        pltpu.VMEM((2,) * (bits - 1) + (rows, width), BF16),
        pltpu.VMEM((2,) * (bits - 1) + (rows, width), BF16),
    ]
    for low, high in ((0, middle), (middle, width)):
        for kind in range(2):
            for left in range(bits - 2, -1, -1):
                shapes.append(pltpu.VMEM((2,) * left + (rows, high - low), BF16))
    shapes.append(pltpu.SemaphoreType.DMA((2, 2 * bits - 1)))
    return shapes


def scatter_of(bits, source, scratch):
    result, inbox, total = scratch[:3]
    width = result.shape[1]
    middle = width // (2 * LANES) * LANES
    each = bits - 1
    refs = scratch[3:-1]
    streams = []
    for s, (low, high) in enumerate(((0, middle), (middle, width))):
        part = refs[2 * each * s : 2 * each * (s + 1)]
        streams.append((low, high, part[:each], part[each:]))
    return Scatter(bits, source, result, inbox, total, streams, scratch[-1])


def project_kernel(
    n, heads, dk, dv,
    x_ref, grad_ref, gain_ref, wq_ref, wk_ref, wv_ref, wg_ref, wdb_ref, *rest
):
    consts = rest[:7]
    xn_ref, gfull_ref, q_ref, k_ref, v_ref, gate_ref, db_ref = rest[7:14]
    outs = rest[14:19]
    scratch = rest[19:23]
    xsend, xrecv, gsend, grecv = rest[23:]
    ring = Ring(n)
    count = x_ref.shape[0]
    x = x_ref[...].astype(F32)
    rate = lax.rsqrt(jnp.mean(x * x, axis=-1, keepdims=True) + EPS_NORM)
    xn_ref[ring.me] = (x * rate * gain_ref[...]).astype(BF16)
    gfull_ref[ring.me] = grad_ref[...]
    enter(ring.targets())
    copies = ring.share(xn_ref, xsend, xrecv)

    def project(index):
        rows = rows_of(index, count)
        chunk = xn_ref[index]
        for w, out in (
            (wq_ref, q_ref), (wk_ref, k_ref), (wv_ref, v_ref), (wg_ref, gate_ref), (wdb_ref, db_ref)
        ):
            out[rows, :] = dot(chunk, w[...])

    project(ring.me)
    for k in ring.steps:
        copies[k].wait_recv()
        project(ring.source(k))
    shares = ring.share(gfull_ref, gsend, grecv)
    mixer_forward_kernel(
        heads, dk, dv, q_ref, k_ref, v_ref, gate_ref, db_ref, *consts, *outs, *scratch
    )
    for k in ring.steps:
        copies[k].wait_send()
        shares[k].wait()


def project_mix(n, heads, x, grad, gain, wq, wk, wv, wg, wdb, *consts):
    count, width = x.shape
    length = count * n
    dk, dv = wq.shape[1] // heads, wv.shape[1] // heads
    pairs = heads * (length // GROUP)
    f32 = lambda *shape: jax.ShapeDtypeStruct(shape, F32)
    shapes = (
        jax.ShapeDtypeStruct((n, count, width), BF16),
        jax.ShapeDtypeStruct((n, count, width), BF16),
        f32(length, heads * dk), f32(length, heads * dk), f32(length, heads * dv),
        f32(length, heads * dv), f32(length, LANES),
        jax.ShapeDtypeStruct((length, heads * dv), BF16),
        f32(pairs, GROUP, GROUP), f32(length, heads * dv), f32(pairs, dk, dv),
        f32(length, heads * dv),
    )
    dma = pltpu.SemaphoreType.DMA((n - 1,))
    return pl.pallas_call(
        partial(project_kernel, n, heads, dk, dv),
        out_shape=shapes,
        in_specs=vmem_specs(15),
        out_specs=tuple(vmem_specs(12)),
        scratch_shapes=[
            pltpu.VMEM((length, heads * dk), F32), pltpu.VMEM((length, heads * dk), F32),
            pltpu.VMEM((length, heads * dv), F32), pltpu.VMEM((heads, dk, dv), F32),
            dma, dma, dma, dma,
        ],
        compiler_params=pltpu.CompilerParams(
            collective_id=0, has_side_effects=True, vmem_limit_bytes=VMEM_BYTES
        ),
        name="project_mix",
    )(x, grad, gain, wq, wk, wv, wg, wdb, *consts)


def middle_kernel(
    n, pad,
    gated_ref, x_ref, grad_ref, gfull_ref, wout_ref, gain_ref, wfg_ref, wfu_ref, wfd_ref,
    resid_ref, dresid_ref, ffn_ref, dgated_ref, joined_ref, gfgain_ref,
    out_send, out_recv, hn, dh_send, dh_recv, dres, d_act, act, d_in, d_val,
    sems,
):
    ring = Ring(n)
    count, width = x_ref.shape
    columns = wfg_ref.shape[1]
    enter(ring.targets())
    sends = {}
    for k in ring.steps:
        out_send[k - 1] = dot(gated_ref[rows_of(ring.to(k), count), :], wout_ref[...]).astype(BF16)
        sends[k] = ring.copy(k, out_send.at[k - 1], out_recv.at[k - 1], sems.at[0], sems.at[1])
        sends[k].start()
    resid = x_ref[...].astype(F32) + dot(gated_ref[rows_of(ring.me, count), :], wout_ref[...])
    for i in range(n):
        d_act[i] = dot(gfull_ref[i], wfd_ref[...], NT)
    for k in ring.steps:
        sends[k].wait_recv()
        resid = resid + out_recv[k - 1].astype(F32)
    resid_ref[...] = resid
    rate = lax.rsqrt(jnp.mean(resid * resid, axis=-1, keepdims=True) + EPS_NORM)
    hn[ring.me] = (resid * rate * gain_ref[...]).astype(BF16)
    shares = ring.share(hn, sems.at[2], sems.at[3])

    def feed(index):
        chunk = hn[index]
        up_in = dot(chunk, wfg_ref[...])
        up_val = dot(chunk, wfu_ref[...])
        sig = sigmoid(up_in)
        d_chunk = d_act[index]
        half = up_in * sig
        act[index] = (half * up_val).astype(BF16)
        d_in[index] = (d_chunk * up_val * sig * (1.0 + up_in * (1.0 - sig))).astype(BF16)
        d_val[index] = (d_chunk * half).astype(BF16)
        return dot(d_in[index], wfg_ref[...], NT) + dot(d_val[index], wfu_ref[...], NT)

    d_hnorm = feed(ring.me)
    returns = {}
    for k in ring.steps:
        shares[k].wait_recv()
        source = ring.source(k)
        back = n - k
        dh_send[back - 1] = feed(source).astype(BF16)
        returns[back] = ring.copy(
            back, dh_send.at[back - 1], dh_recv.at[back - 1], sems.at[4], sems.at[5]
        )
        returns[back].start()
    flat = lambda ref: ref[...].reshape(n * count, ref.shape[2])
    padded = columns + (-columns % LANES)
    for i, (left, right) in enumerate(((hn, d_in), (hn, d_val), (gfull_ref, act))):
        if padded > columns:
            joined_ref[:, i * padded + padded - LANES : (i + 1) * padded] = jnp.zeros(
                (width, LANES), BF16
            )
        value = flat(right)
        lhs = flat(left)
        for base in range(0, width, pad):
            joined_ref[base : base + pad, i * padded : i * padded + columns] = dot(
                lhs[:, base : base + pad], value, TN
            ).astype(BF16)
    for i in range(n):
        ffn_ref[i * count : (i + 1) * count, :] = dot(act[i], wfd_ref[...]).astype(BF16)
    for k in ring.steps:
        returns[k].wait_recv()
        d_hnorm = d_hnorm + dh_recv[k - 1].astype(F32)
    plain = resid_ref[...] * rate
    gfgain_ref[...] = jnp.sum(d_hnorm * plain, axis=0, keepdims=True)
    up = d_hnorm * gain_ref[...]
    d_resid = grad_ref[...].astype(F32) + rate * (
        up - plain * jnp.mean(up * plain, axis=-1, keepdims=True)
    )
    dresid_ref[...] = d_resid
    dres[ring.me] = d_resid.astype(BF16)
    spread = ring.share(dres, sems.at[6], sems.at[7])
    dgated_ref[rows_of(ring.me, count), :] = dot(dres[ring.me], wout_ref[...], NT)
    for k in ring.steps:
        spread[k].wait_recv()
        source = ring.source(k)
        dgated_ref[rows_of(source, count), :] = dot(dres[source], wout_ref[...], NT)
    lhs, value = flat(dres), gated_ref[...]
    for base in range(0, width, pad):
        joined_ref[base : base + pad, 3 * padded :] = dot(
            lhs[:, base : base + pad], value, TN
        ).astype(BF16)
    for group in (sends, shares, returns, spread):
        for k in ring.steps:
            group[k].wait_send()


def middle(n, gated, x, grad, gfull, wout, gain, wfg, wfu, wfd):
    count, width = x.shape
    length = n * count
    inner, columns = wout.shape[0], wfg.shape[1]
    padded = columns + (-columns % LANES)
    f32 = lambda *shape: jax.ShapeDtypeStruct(shape, F32)
    slots = pltpu.VMEM((n - 1, count, width), BF16)
    return pl.pallas_call(
        partial(middle_kernel, n, math.gcd(width, 256)),
        out_shape=(
            f32(count, width), f32(count, width),
            jax.ShapeDtypeStruct((length, width), BF16),
            f32(length, inner),
            jax.ShapeDtypeStruct((width, 3 * padded + inner), BF16),
            f32(1, width),
        ),
        in_specs=vmem_specs(9),
        out_specs=tuple(vmem_specs(6)),
        scratch_shapes=[
            slots, slots, pltpu.VMEM((n, count, width), BF16), slots, slots,
            pltpu.VMEM((n, count, width), BF16),
            pltpu.VMEM((n, count, columns), F32),
            pltpu.VMEM((n, count, columns), BF16),
            pltpu.VMEM((n, count, columns), BF16),
            pltpu.VMEM((n, count, columns), BF16),
            pltpu.SemaphoreType.DMA((8, n - 1)),
        ],
        compiler_params=pltpu.CompilerParams(
            collective_id=1, has_side_effects=True, vmem_limit_bytes=VMEM_BYTES
        ),
        name="middle",
    )(gated, x, grad, gfull, wout, gain, wfg, wfu, wfd)


def back_kernel(n, bits, heads, dk, dv, columns, *refs):
    mixer_in, (joined_ref, ffn_ref, resid_ref) = refs[:17], refs[17:20]
    mixer_out, (block_ref, sgate_ref, sup_ref, sdown_ref, sout_ref) = refs[20:26], refs[26:31]
    mixer_scratch, (boxes, fsems), scratch = refs[31:41], refs[41:43], refs[43:]
    ring = Ring(n)
    scatter = scatter_of(bits, joined_ref, scratch)
    enter(ring.targets() + scatter.targets())
    scatter.step(0)
    count = resid_ref.shape[0]
    sends = {}
    for k in ring.steps:
        sends[k] = ring.copy(
            k, ffn_ref.at[rows_of(ring.to(k), count), :], boxes.at[k - 1], fsems.at[0], fsems.at[1]
        )
        sends[k].start()
    mixer_backward_kernel(heads, dk, dv, *mixer_in, *mixer_out, *mixer_scratch, tick=scatter.step)
    for phase in range(3, bits + 1):
        scatter.step(phase)
    block = resid_ref[...] + ffn_ref[rows_of(ring.me, count), :].astype(F32)
    for k in ring.steps:
        sends[k].wait_recv()
        block = block + boxes[k - 1].astype(F32)
    block_ref[...] = block.astype(BF16)
    result = scratch[0]
    padded = columns + (-columns % LANES)
    sgate_ref[...] = result[:, :columns]
    sup_ref[...] = result[:, padded : padded + columns]
    sdown_ref[...] = result[:, 2 * padded : 3 * padded].T[:columns, :]
    sout_ref[...] = result[:, 3 * padded :].T
    for k in ring.steps:
        sends[k].wait_send()
    scatter.finish()


def backward(n, bits, heads, columns, mixer_in, joined, ffn, resid):
    q, v = mixer_in[0], mixer_in[2]
    length = q.shape[0]
    dk, dv = q.shape[1] // heads, v.shape[1] // heads
    wide_out = 2 * heads * dk + 2 * heads * dv + LANES
    count, width = resid.shape
    size = 1 << bits
    rows = joined.shape[0] // size
    f32 = lambda *shape: jax.ShapeDtypeStruct(shape, F32)
    inner = joined.shape[1] - 3 * (columns + (-columns % LANES))
    shapes = (
        jax.ShapeDtypeStruct((length, wide_out), BF16),
        f32(*mixer_in[7].shape), f32(*mixer_in[8].shape), f32(*mixer_in[9].shape),
        f32(1, LANES), f32(1, dv),
        jax.ShapeDtypeStruct((count, width), BF16),
        f32(rows, columns), f32(rows, columns), f32(columns, rows), f32(inner, rows),
    )
    narrow, broad = (length, heads * dk), (length, heads * dv)
    cubed = joined.reshape((2,) * bits + (rows, joined.shape[1]))
    return pl.pallas_call(
        partial(back_kernel, n, bits, heads, dk, dv, columns),
        out_shape=shapes,
        in_specs=vmem_specs(20),
        out_specs=tuple(vmem_specs(11)),
        scratch_shapes=[
            pltpu.VMEM(narrow, F32), pltpu.VMEM(narrow, F32), pltpu.VMEM(broad, F32),
            pltpu.VMEM(broad, F32), pltpu.VMEM(narrow, F32), pltpu.VMEM(narrow, F32),
            pltpu.VMEM(broad, F32), pltpu.VMEM((heads, dk, dv), F32),
            pltpu.VMEM((length, LANES), F32), pltpu.VMEM((length, LANES), F32),
            pltpu.VMEM((n - 1, count, width), BF16), pltpu.SemaphoreType.DMA((2, n - 1)),
        ] + scatter_scratch(bits, rows, joined.shape[1]),
        compiler_params=pltpu.CompilerParams(
            collective_id=2, has_side_effects=True, vmem_limit_bytes=VMEM_BYTES
        ),
        name="mixer_back",
    )(*mixer_in, cubed, ffn, resid)


def last_kernel(n, bits, heads, dk, dv, *refs):
    (d_ref, xn_ref, x_ref, gain_ref, dresid_ref, wq_ref, wk_ref, wv_ref, wg_ref, wdb_ref,
     gq_ref, gk_ref, gv_ref, grate_ref, gogain_ref, gfgain_ref) = refs[:16]
    (dx_ref, sq_ref, sk_ref, sv_ref, sg_ref, sd_ref, sb_ref,
     cq_ref, ck_ref, cv_ref, rate_ref, again_ref, ogain_ref, fgain_ref) = refs[16:30]
    grads, dx_send, dx_recv, gains, small, small_in, sems, small_sems = refs[30:38]
    scratch = refs[38:]
    ring = Ring(n)
    scatter = scatter_of(bits, grads, scratch)
    enter(ring.targets() + scatter.targets())
    count, width = x_ref.shape
    weights = (wq_ref, wk_ref, wv_ref, wg_ref, wdb_ref)

    def back_rows(index):
        rows = rows_of(index, count)
        base, total = 0, None
        for w in weights:
            part = dot(d_ref[rows, base : base + w.shape[1]], w[...], NT)
            total = part if total is None else total + part
            base += w.shape[1]
        return total, jnp.sum(total * xn_ref[index].astype(F32), axis=0, keepdims=True)

    d_xnorm, g_again = back_rows(ring.me)
    for k in ring.steps:
        total, part = back_rows(ring.to(k))
        dx_send[k - 1] = total.astype(BF16)
        g_again = g_again + part
    span = gains.shape[2]
    gains[ring.me] = jnp.zeros((8, span), F32)
    gains[ring.me, 0:1, :width] = g_again / gain_ref[...]
    gains[ring.me, 1:2, :width] = gfgain_ref[...]
    gains[ring.me, 2:3, :dv] = gogain_ref[...]
    shares = ring.share(gains, sems.at[0], sems.at[1])
    sends = {}
    for k in ring.steps:
        sends[k] = ring.copy(k, dx_send.at[k - 1], dx_recv.at[k - 1], sems.at[2], sems.at[3])
        sends[k].start()
    lhs = xn_ref[...].reshape(n * count, width)
    rows = width // (1 << bits)
    step = max(rows, 256)
    for base in range(0, width, step):
        value = dot(lhs[:, base : base + step], d_ref[...], TN).astype(BF16)
        for inner in range(0, step, rows):
            block = (base + inner) // rows
            lead = tuple((block >> b) % 2 for b in range(bits - 1, -1, -1))
            grads[lead] = value[inner : inner + rows]
    scatter.step(0)
    small[0] = jnp.zeros(small.shape[1:], F32)
    narrow, broad = heads * dk, heads * dv
    taps = gq_ref.shape[0]
    small[0, 0:taps, :narrow] = gq_ref[...]
    small[0, 0:taps, narrow : 2 * narrow] = gk_ref[...]
    small[0, 0:taps, 2 * narrow : 2 * narrow + broad] = gv_ref[...]
    small[0, 8:9, :LANES] = grate_ref[...]
    for k in ring.steps:
        shares[k].wait_recv()
    total = gains[0]
    for i in range(1, n):
        total = total + gains[i]
    small[0, 16:24, :] = total
    swaps = []

    def swap(b):
        copy = pltpu.make_async_remote_copy(
            src_ref=small.at[b], dst_ref=small_in.at[b],
            send_sem=small_sems.at[0, b], recv_sem=small_sems.at[1, b],
            device_id=scatter.partner(b), device_id_type=MESH,
        )
        copy.start()
        swaps.append(copy)

    for b in range(bits):
        swap(b)
        scatter.step(b + 1)
        swaps[b].wait_recv()
        small[b + 1] = small[b] + small_in[b]
    final = small.at[bits]
    cq_ref[...] = final[0:taps, :narrow]
    ck_ref[...] = final[0:taps, narrow : 2 * narrow]
    cv_ref[...] = final[0:taps, 2 * narrow : 2 * narrow + broad]
    rate_ref[...] = final[8:9, :LANES]
    again_ref[...] = final[16:17, :width]
    fgain_ref[...] = final[17:18, :width]
    ogain_ref[...] = final[18:19, :dv]
    result = scratch[0]
    sq_ref[...] = result[:, :narrow]
    sk_ref[...] = result[:, narrow : 2 * narrow]
    base = 2 * narrow
    sv_ref[...] = result[:, base : base + broad]
    sg_ref[...] = result[:, base + broad : base + 2 * broad]
    base = base + 2 * broad
    sd_ref[...] = result[:, base : base + heads]
    sb_ref[...] = result[:, base + heads : base + 2 * heads]
    for k in ring.steps:
        sends[k].wait_recv()
        d_xnorm = d_xnorm + dx_recv[k - 1].astype(F32)
    x = x_ref[...].astype(F32)
    rate = lax.rsqrt(jnp.mean(x * x, axis=-1, keepdims=True) + EPS_NORM)
    plain = x * rate
    up = d_xnorm * gain_ref[...]
    dx_ref[...] = (
        dresid_ref[...] + rate * (up - plain * jnp.mean(up * plain, axis=-1, keepdims=True))
    ).astype(BF16)
    for k in ring.steps:
        shares[k].wait_send()
        sends[k].wait_send()
    for copy in swaps:
        copy.wait_send()
    scatter.finish()


def last(n, bits, heads, *args):
    d_cat, xn, x, _, _, wq, _, wv = args[:8]
    taps = args[10].shape[0]
    narrow, broad = wq.shape[1], wv.shape[1]
    dk, dv = narrow // heads, broad // heads
    count, width = x.shape
    rows = width >> bits
    span = max(width, 2 * narrow + broad)
    f32 = lambda *shape: jax.ShapeDtypeStruct(shape, F32)
    slots = pltpu.VMEM((n - 1, count, width), BF16)
    return pl.pallas_call(
        partial(last_kernel, n, bits, heads, dk, dv),
        out_shape=(
            jax.ShapeDtypeStruct((count, width), BF16),
            f32(rows, narrow), f32(rows, narrow), f32(rows, broad), f32(rows, broad),
            f32(rows, heads), f32(rows, heads),
            f32(taps, narrow), f32(taps, narrow), f32(taps, broad), f32(1, LANES),
            f32(1, width), f32(1, dv), f32(1, width),
        ),
        in_specs=vmem_specs(16),
        out_specs=tuple(vmem_specs(14)),
        scratch_shapes=[
            pltpu.VMEM((2,) * bits + (rows, d_cat.shape[1]), BF16),
            slots, slots,
            pltpu.VMEM((n, 8, span), F32),
            pltpu.VMEM((bits + 1, 24, span), F32),
            pltpu.VMEM((bits, 24, span), F32),
            pltpu.SemaphoreType.DMA((4, n - 1)),
            pltpu.SemaphoreType.DMA((2, bits)),
        ] + scatter_scratch(bits, rows, d_cat.shape[1]),
        compiler_params=pltpu.CompilerParams(
            collective_id=3, has_side_effects=True, vmem_limit_bytes=VMEM_BYTES
        ),
        name="last",
    )(*args)


def body(
    n,
    bits,
    tokens,
    seg_ids,
    attn_gain,
    w_query,
    w_key,
    w_value,
    w_gate,
    w_decay,
    w_beta,
    conv_query,
    conv_key,
    conv_value,
    decay_rate,
    out_gain,
    w_out,
    ffn_gain,
    w_ffn_gate,
    w_ffn_up,
    w_ffn_down,
    grad_out,
):
    heads = w_decay.shape[1]
    row = lambda array: array.reshape(1, -1)
    w_db = jnp.concatenate(
        [w_decay, w_beta, jnp.zeros((w_decay.shape[0], LANES - 2 * heads), BF16)], axis=1
    )
    rate_row = row(jnp.pad(decay_rate, (0, LANES - heads)))
    consts = (
        seg_ids.reshape(-1, 1), seg_ids, conv_query, conv_key, conv_value, rate_row, row(out_gain)
    )
    xnorm, grad_full, *projs, gated, inv, delta, states, mixed = project_mix(
        n, heads, tokens, grad_out, row(attn_gain), w_query, w_key, w_value, w_gate, w_db, *consts
    )
    resid, d_resid, ffn, d_gated, joined, g_fgain = middle(
        n, gated, tokens, grad_out, grad_full, w_out, row(ffn_gain), w_ffn_gate, w_ffn_up, w_ffn_down
    )
    mixer_in = (*projs, *consts, inv, delta, states, mixed, d_gated)
    d_cat, g_cq, g_ck, g_cv, g_rate, g_ogain, block_out, s_fgate, s_fup, s_down, s_out = backward(
        n, bits, heads, w_ffn_gate.shape[1], mixer_in, joined, ffn, resid
    )
    (grad_tokens, s_query, s_key, s_value, s_gate, s_decay, s_beta,
     g_cq, g_ck, g_cv, g_rate, g_again, g_ogain, g_fgain) = last(
        n, bits, heads, d_cat, xnorm, tokens, row(attn_gain), d_resid,
        w_query, w_key, w_value, w_gate, w_db, g_cq, g_ck, g_cv, g_rate, g_ogain, g_fgain
    )
    flat = lambda array: array.reshape(-1)
    return (
        block_out, grad_tokens, flat(g_again), s_query, s_key, s_value, s_gate, s_decay, s_beta,
        g_cq, g_ck, g_cv, flat(g_rate)[:heads], flat(g_ogain), s_out, flat(g_fgain),
        s_fgate, s_fup, s_down,
    )


def solution(mesh):
    in_specs = (
        P(("dp", "tensor"), None),
        P("dp", None),
        P(),
        P(None, "tensor"),
        P(None, "tensor"),
        P(None, "tensor"),
        P(None, "tensor"),
        P(None, "tensor"),
        P(None, "tensor"),
        P(None, "tensor"),
        P(None, "tensor"),
        P(None, "tensor"),
        P("tensor"),
        P(),
        P("tensor", None),
        P(),
        P(None, "tensor"),
        P(None, "tensor"),
        P("tensor", None),
        P(("dp", "tensor"), None),
    )
    out_specs = (
        P(("dp", "tensor"), None),
        P(("dp", "tensor"), None),
        P(),
        P("dp", "tensor"),
        P("dp", "tensor"),
        P("dp", "tensor"),
        P("dp", "tensor"),
        P("dp", "tensor"),
        P("dp", "tensor"),
        P(None, "tensor"),
        P(None, "tensor"),
        P(None, "tensor"),
        P("tensor"),
        P(),
        P("tensor", "dp"),
        P(),
        P("dp", "tensor"),
        P("dp", "tensor"),
        P("tensor", "dp"),
    )
    n = mesh.shape["tensor"]
    bits = mesh.shape["dp"].bit_length() - 1
    return jax.shard_map(partial(body, n, bits), mesh=mesh, in_specs=in_specs, out_specs=out_specs, check_vma=False)
```

```python
from functools import partial
import math

import jax
import jax.numpy as jnp
from jax import lax
from jax.experimental import pallas as pl
from jax.experimental.pallas import tpu as pltpu
from jax.sharding import PartitionSpec as P

GROUP = 64
LANES = 128
EPS_NORM = 1e-05
EPS_UNIT = 1e-06
HIGHEST = lax.Precision.HIGHEST
HIGH = lax.Precision.HIGH
F32 = jnp.float32
BF16 = jnp.bfloat16
MESH = pl.DeviceIdType.MESH
NN = (((1,), (0,)), ((), ()))
NT = (((1,), (1,)), ((), ()))
TN = (((0,), (0,)), ((), ()))
VMEM_BYTES = 56 << 20


def dot(a, b, dims=NN):
    return lax.dot_general(a.astype(BF16), b.astype(BF16), dims, preferred_element_type=F32)


def dot_fine(a, b, dims=NN):
    return lax.dot_general(a, b, dims, precision=HIGH, preferred_element_type=F32)


def shift_down(values, offset, keep):
    return pltpu.roll(values, offset, 0) * keep


def shift_up(values, offset, keep):
    rolled = values * keep
    return pltpu.roll(rolled, values.shape[0] - offset, 0)


def spread_lanes(seg_row):
    return jnp.broadcast_to(seg_row, (LANES, seg_row.shape[1])).T


def conv_keeps(seg, taps):
    length = seg.shape[0]
    row = lax.broadcasted_iota(jnp.int32, (length, LANES), 0)
    keeps = []
    for offset in range(1, taps):
        same = (seg == pltpu.roll(seg, offset, 0)) & (row >= offset)
        keeps.append(same.astype(F32))
    return keeps


def wide(keep, columns):
    return jnp.concatenate([keep] * (columns // LANES), axis=1) if columns > LANES else keep


def conv(values, taps, keeps):
    total = taps[0:1] * values
    for offset in range(1, taps.shape[0]):
        total = total + taps[offset : offset + 1] * shift_down(
            values, offset, wide(keeps[offset - 1], values.shape[1])
        )
    return total


def conv_back(values, taps, keeps, d_out):
    d_values = taps[0:1] * d_out
    d_taps = [jnp.sum(values * d_out, axis=0, keepdims=True)]
    for offset in range(1, taps.shape[0]):
        keep = wide(keeps[offset - 1], values.shape[1])
        moved = shift_up(d_out, offset, keep)
        d_values = d_values + taps[offset : offset + 1] * moved
        d_taps.append(jnp.sum(values * moved, axis=0, keepdims=True))
    return d_values, jnp.concatenate(d_taps, axis=0)


def softplus(values):
    return jnp.maximum(values, 0.0) + jnp.log1p(jnp.exp(-jnp.abs(values)))


def sigmoid(values):
    return jax.nn.sigmoid(values)


def silu_back(values):
    sig = sigmoid(values)
    return sig * (1.0 + values * (1.0 - sig))


def block_cumsum(values):
    length = values.shape[0]
    row = lax.broadcasted_iota(jnp.int32, values.shape, 0) % GROUP
    step = 1
    while step < GROUP:
        values = values + jnp.where(row >= step, pltpu.roll(values, step, 0), 0.0)
        step *= 2
    return values


def block_cumsum_back(values):
    length = values.shape[0]
    row = lax.broadcasted_iota(jnp.int32, values.shape, 0) % GROUP
    step = 1
    while step < GROUP:
        values = values + jnp.where(
            row < GROUP - step, pltpu.roll(values, length - step, 0), 0.0
        )
        step *= 2
    return values


def invert(lowers):
    size = lowers[0].shape[0]
    rows = lax.broadcasted_iota(jnp.int32, (size, size), 0)
    cols = lax.broadcasted_iota(jnp.int32, (size, size), 1)
    eye = (rows == cols).astype(F32)
    pair = (rows // 2 == cols // 2).astype(F32)
    done = [eye - low * pair for low in lowers]
    half = 2
    while half < size:
        keep = (rows // (2 * half) == cols // (2 * half)) & (rows // half != cols // half)
        keep = keep.astype(F32)
        steps = [dot_fine(low * keep, inv) for low, inv in zip(lowers, done)]
        done = [inv - dot_fine(inv, step) for inv, step in zip(done, steps)]
        half *= 2
    return done


def block_masks(seg_col, seg_row, cum, cum_t, n, h):
    rows = slice(n * GROUP, (n + 1) * GROUP)
    index_t = lax.broadcasted_iota(jnp.int32, (GROUP, GROUP), 0)
    index_i = lax.broadcasted_iota(jnp.int32, (GROUP, GROUP), 1)
    doc_col = seg_col[rows]
    doc_row = seg_row[:, rows]
    c_col = cum[rows, h : h + 1]
    c_row = cum_t[h : h + 1, rows]
    c_last = c_col[GROUP - 1 : GROUP]
    same = ((doc_col == doc_row) & (index_t >= index_i)).astype(F32)
    spread = jnp.exp(jnp.minimum(c_col - c_row, 0.0)) * same
    strict = (index_t > index_i).astype(F32)
    end_doc = doc_col[GROUP - 1 : GROUP]
    late = jnp.exp(jnp.minimum(c_last - c_col, 0.0)) * (doc_col == end_doc).astype(F32)
    if n == 0:
        carried = jnp.zeros_like(c_col)
    else:
        prev = seg_col[n * GROUP - 1 : n * GROUP]
        carried = jnp.exp(c_col) * (doc_col == prev).astype(F32)
    return spread, strict, late, carried


def unit(values):
    rate = lax.rsqrt(jnp.sum(values * values, axis=-1, keepdims=True) + EPS_UNIT)
    return values * rate, rate


def mixer_forward_kernel(
    heads, dk, dv,
    q_ref, k_ref, v_ref, gate_ref, db_ref, seg_row_ref,
    tq_ref, tk_ref, tv_ref, rate_ref, ogain_ref,
    gated_ref, inv_ref, delta_ref, state_ref, mixed_ref,
    query, keys, values, carry, tick=None,
):
    length = q_ref.shape[0]
    blocks = length // GROUP
    seg_row = seg_row_ref[...].astype(F32)
    seg_wide = spread_lanes(seg_row)
    seg_col = seg_wide[:, :1]
    keeps = conv_keeps(seg_wide, tq_ref.shape[0])
    db = db_ref[...]
    beta = sigmoid(db)
    cum = block_cumsum(-rate_ref[...] * softplus(db))
    cum_t = cum.T
    scale = 1.0 / math.sqrt(dk)
    for h in range(heads):
        cols = slice(h * dk, (h + 1) * dk)
        query[:, cols] = unit(jax.nn.silu(conv(q_ref[:, cols], tq_ref[:, cols], keeps)))[0] * scale
        keys[:, cols] = unit(jax.nn.silu(conv(k_ref[:, cols], tk_ref[:, cols], keeps)))[0]
        cols = slice(h * dv, (h + 1) * dv)
        values[:, cols] = jax.nn.silu(conv(v_ref[:, cols], tv_ref[:, cols], keeps))

    tick(1)
    lowers = []
    for n in range(blocks):
        rows = slice(n * GROUP, (n + 1) * GROUP)
        for h in range(heads):
            key = keys[rows, h * dk : (h + 1) * dk]
            spread, strict, late, carried = block_masks(seg_col, seg_row, cum, cum_t, n, h)
            b = beta[rows, heads + h : heads + h + 1]
            lowers.append(b * dot_fine(key, key, NT) * spread * strict)
    for i, inv in enumerate(invert(lowers)):
        inv_ref[i] = inv
    tick(2)

    for h in range(heads):
        carry[h] = jnp.zeros((dk, dv), F32)
    for n in range(blocks):
        rows = slice(n * GROUP, (n + 1) * GROUP)
        for h in range(heads):
            pair = n * heads + h
            kc, vc = slice(h * dk, (h + 1) * dk), slice(h * dv, (h + 1) * dv)
            key, q, v = keys[rows, kc], query[rows, kc], values[rows, vc]
            spread, strict, late, carried = block_masks(seg_col, seg_row, cum, cum_t, n, h)
            b = beta[rows, heads + h : heads + h + 1]
            inv = inv_ref[pair]
            fresh = dot(inv, b * v)
            state = carry[h]
            state_ref[pair] = state
            if n == 0:
                delta = fresh
            else:
                delta = fresh - dot(dot(inv, (b * carried) * key), state)
            delta_ref[rows, vc] = delta
            mixed = dot(dot(q, key, NT) * spread, delta)
            if n > 0:
                mixed = mixed + dot(q * carried, state)
            mixed_ref[rows, vc] = mixed
            if n < blocks - 1:
                new = dot(key * late, delta, TN)
                if n > 0:
                    new = new + carried[GROUP - 1 : GROUP] * state
                carry[h] = new
    for h in range(heads):
        vc = slice(h * dv, (h + 1) * dv)
        mixed = mixed_ref[:, vc]
        rate = lax.rsqrt(jnp.mean(mixed * mixed, axis=-1, keepdims=True) + EPS_NORM)
        gated_ref[:, vc] = (mixed * rate * ogain_ref[...] * jax.nn.silu(gate_ref[:, vc])).astype(BF16)


def vmem_specs(count):
    return [pl.BlockSpec(memory_space=pltpu.VMEM)] * count


def mixer_backward_kernel(
    heads, dk, dv,
    q_ref, k_ref, v_ref, gate_ref, db_ref, seg_row_ref,
    tq_ref, tk_ref, tv_ref, rate_ref, ogain_ref,
    inv_ref, delta_ref, state_ref, mixed_ref, dgated_ref,
    d_ref, gq_ref, gk_ref, gv_ref, grate_ref, gogain_ref,
    keys, query, values, d_mixed, d_key, d_query, d_value, d_carry, d_cum, d_beta,
    tick=None,
):
    length = q_ref.shape[0]
    blocks = length // GROUP
    seg_row = seg_row_ref[...].astype(F32)
    seg_wide = spread_lanes(seg_row)
    seg_col = seg_wide[:, :1]
    keeps = conv_keeps(seg_wide, tq_ref.shape[0])
    db = db_ref[...]
    beta = sigmoid(db)
    rate_row = rate_ref[...]
    soft = softplus(db)
    cum = block_cumsum(-rate_row * soft)
    cum_t = cum.T
    scale = 1.0 / math.sqrt(dk)
    v_base = 2 * heads * dk
    g_base = v_base + heads * dv
    b_base = g_base + heads * dv

    g_ogain = jnp.zeros((1, dv), F32)
    for h in range(heads):
        vc = slice(h * dv, (h + 1) * dv)
        mixed = mixed_ref[:, vc]
        gate = gate_ref[:, vc]
        dg = dgated_ref[:, vc]
        rate = lax.rsqrt(jnp.mean(mixed * mixed, axis=-1, keepdims=True) + EPS_NORM)
        plain = mixed * rate
        sig = sigmoid(gate)
        d_norm = dg * gate * sig
        d_ref[:, g_base + h * dv : g_base + (h + 1) * dv] = (
            dg * plain * ogain_ref[...] * sig * (1.0 + gate * (1.0 - sig))
        ).astype(BF16)
        g_ogain = g_ogain + jnp.sum(d_norm * plain, axis=0, keepdims=True)
        up = d_norm * ogain_ref[...]
        d_mixed[:, vc] = rate * (up - plain * jnp.mean(up * plain, axis=-1, keepdims=True))
        kc = slice(h * dk, (h + 1) * dk)
        query[:, kc] = unit(jax.nn.silu(conv(q_ref[:, kc], tq_ref[:, kc], keeps)))[0] * scale
        keys[:, kc] = unit(jax.nn.silu(conv(k_ref[:, kc], tk_ref[:, kc], keeps)))[0]
        values[:, vc] = jax.nn.silu(conv(v_ref[:, vc], tv_ref[:, vc], keeps))
        d_carry[h] = jnp.zeros((dk, dv), F32)
    gogain_ref[...] = g_ogain
    tick(0)

    lane = lax.broadcasted_iota(jnp.int32, (GROUP, LANES), 1)
    row_col = lax.broadcasted_iota(jnp.int32, (GROUP, 1), 0)
    index_t = lax.broadcasted_iota(jnp.int32, (GROUP, GROUP), 0)
    index_i = lax.broadcasted_iota(jnp.int32, (GROUP, GROUP), 1)
    eye = (index_t == index_i).astype(F32)
    for n in reversed(range(blocks)):
        if n == blocks // 2 - 1:
            tick(1)
        rows = slice(n * GROUP, (n + 1) * GROUP)
        dc_block = jnp.zeros((GROUP, LANES), F32)
        db_block = jnp.zeros((GROUP, LANES), F32)
        last = n == blocks - 1
        for h in range(heads):
            pair = n * heads + h
            kc, vc = slice(h * dk, (h + 1) * dk), slice(h * dv, (h + 1) * dv)
            key, q, v = keys[rows, kc], query[rows, kc], values[rows, vc]
            spread, strict, late, a = block_masks(seg_col, seg_row, cum, cum_t, n, h)
            b = beta[rows, heads + h : heads + h + 1]
            inv = inv_ref[pair]
            delta = delta_ref[rows, vc]
            state = state_ref[pair]
            d_out = d_mixed[rows, vc]
            d_next = d_carry[h]
            key_late = key * late
            gram = dot(key, key, NT)
            score = dot(q, key, NT)
            d_score = dot(d_out, delta, NT)
            d_delta = dot(score * spread, d_out, TN)
            if not last:
                d_delta = d_delta + dot(key_late, d_next)
            d_right = dot(inv, d_delta, TN)
            d_lower = -dot(d_right, delta, NT) * strict
            d_value[rows, vc] = b * d_right
            dk_sum = jnp.zeros((GROUP, dk), F32)
            dq_sum = jnp.zeros((GROUP, dk), F32)
            d_b = jnp.sum(d_right * v, axis=-1, keepdims=True)
            d_c = jnp.zeros((GROUP, 1), F32)
            if n > 0:
                d_from = (-b * a) * d_right
                from_state = dot(key, state)
                d_b = d_b - a * jnp.sum(d_right * from_state, axis=-1, keepdims=True)
                dk_sum = dk_sum + dot(d_from, state, NT)
                reads = dot(d_out, state, NT)
                dq_sum = dq_sum + a * reads
                d_a = jnp.sum(q * reads, axis=-1, keepdims=True) - b * jnp.sum(
                    d_right * from_state, axis=-1, keepdims=True
                )
                d_state = dot(q * a, d_out, TN) + dot(key, d_from, TN)
                if not last:
                    a_last = a[GROUP - 1 : GROUP]
                    d_state = d_state + a_last * d_next
                    d_a = d_a + jnp.where(
                        row_col == GROUP - 1,
                        jnp.sum(jnp.sum(state * d_next, axis=-1, keepdims=True), axis=0, keepdims=True),
                        0.0,
                    )
                d_carry[h] = d_state
                d_c = d_c + d_a * a
            if not last:
                d_late_key = dot(delta, d_next, NT)
                dk_sum = dk_sum + late * d_late_key
                d_late = late * jnp.sum(key * d_late_key, axis=-1, keepdims=True)
                d_c = d_c - d_late + jnp.where(
                    row_col == GROUP - 1, jnp.sum(d_late, axis=0, keepdims=True), 0.0
                )
            d_pair = d_score * spread
            dq_sum = dq_sum + dot(d_pair, key)
            dk_sum = dk_sum + dot(d_pair, q, TN)
            gram_spread = gram * spread
            d_b = d_b + jnp.sum(d_lower * gram_spread, axis=-1, keepdims=True)
            d_gram = d_lower * (b * spread)
            dk_sum = dk_sum + dot(d_gram, key) + dot(d_gram, key, TN)
            cross = d_pair * score + d_gram * gram
            d_c = d_c + jnp.sum(cross, axis=-1, keepdims=True)
            falls = jnp.sum(cross, axis=0, keepdims=True)
            d_c = d_c - jnp.sum(eye * falls, axis=-1, keepdims=True)
            d_key[rows, kc] = dk_sum
            d_query[rows, kc] = dq_sum
            dc_block = dc_block + jnp.where(lane == h, d_c, 0.0)
            db_block = db_block + jnp.where(lane == heads + h, d_b, 0.0)
        d_cum[rows, :] = dc_block
        d_beta[rows, :] = db_block

    tick(2)
    d_log = block_cumsum_back(d_cum[...])
    grate_ref[...] = jnp.sum(d_log * -soft, axis=0, keepdims=True)
    sig = beta
    d_ref[:, b_base : b_base + LANES] = (
        d_log * -rate_row * sig + d_beta[...] * sig * (1.0 - sig)
    ).astype(BF16)

    for h in range(heads):
        kc, vc = slice(h * dk, (h + 1) * dk), slice(h * dv, (h + 1) * dv)
        for ref, taps, g_ref, d_unit, base, factor in (
            (q_ref, tq_ref, gq_ref, d_query, 0, scale),
            (k_ref, tk_ref, gk_ref, d_key, heads * dk, 1.0),
        ):
            proj = ref[:, kc]
            pre = conv(proj, taps[:, kc], keeps)
            act = jax.nn.silu(pre)
            normed, rate = unit(act)
            up = d_unit[:, kc] * factor
            d_act = rate * (up - normed * jnp.sum(up * normed, axis=-1, keepdims=True))
            d_proj, d_taps = conv_back(proj, taps[:, kc], keeps, d_act * silu_back(pre))
            d_ref[:, base + h * dk : base + (h + 1) * dk] = d_proj.astype(BF16)
            g_ref[:, kc] = d_taps
        proj = v_ref[:, vc]
        pre = conv(proj, tv_ref[:, vc], keeps)
        d_proj, d_taps = conv_back(proj, tv_ref[:, vc], keeps, d_value[:, vc] * silu_back(pre))
        d_ref[:, v_base + h * dv : v_base + (h + 1) * dv] = d_proj.astype(BF16)
        gv_ref[:, vc] = d_taps


def rows_of(index, count):
    return pl.ds(pl.multiple_of(index * count, count), count)


def enter(targets):
    barrier = pltpu.get_barrier_semaphore()
    for target in targets:
        pl.semaphore_signal(barrier, inc=1, device_id=target, device_id_type=MESH)
    pl.semaphore_wait(barrier, len(targets))


def order_of(n):
    steps = []
    for k in range(1, n // 2 + 1):
        steps.append(k)
        if n - k != k:
            steps.append(n - k)
    return steps


class Ring:
    def __init__(self, n):
        self.n = n
        self.me = lax.axis_index("tensor")
        self.steps = order_of(n)

    def to(self, k):
        return lax.rem(self.me + k, self.n)

    def source(self, k):
        return lax.rem(self.me + self.n - k, self.n)

    def targets(self):
        return [{"tensor": self.to(k)} for k in self.steps]

    def copy(self, k, src, dst, send, recv):
        return pltpu.make_async_remote_copy(
            src_ref=src, dst_ref=dst, send_sem=send.at[k - 1], recv_sem=recv.at[k - 1],
            device_id={"tensor": self.to(k)}, device_id_type=MESH,
        )

    def share(self, ref, send, recv):
        copies = {}
        for k in self.steps:
            copies[k] = self.copy(k, ref.at[self.me], ref.at[self.me], send, recv)
            copies[k].start()
        return copies


def pick(index, values):
    out = values[0]
    for i in range(1, len(values)):
        out = jnp.where(index == i, values[i], out)
    return out


class Line:
    def __init__(self, n):
        self.n, self.p = n, lax.axis_index("tensor")

    def has(self, side):
        return self.p != jnp.where(side == 0, self.n - 1, 0)

    def fed(self, side):
        return self.has(1 - side)

    def peer(self, side):
        return {"tensor": self.p + 1 - 2 * side}

    def place(self, i, key):
        n = self.n
        table = [sorted(range(n), key=lambda d: (d != p, key(p, d))) for p in range(n)]
        return pick(self.p, [row[i] for row in table])

    def arrival(self, i):
        return self.place(i, lambda p, d: (abs(d - p), d))

    def early(self, i):
        last = self.n - 1
        return self.place(i, lambda p, d: (last - d) + p if d > p else d + (last - p))

    def late(self, i):
        last = self.n - 1
        return self.place(i, lambda p, d: d + p if d > p else (last - d) + (last - p))

    def toward(self, d):
        return jnp.where(d > self.p, 0, 1), jnp.abs(d - self.p) - 1


PARTS = 2


def part_rows(count):
    step = count // PARTS
    return [pl.ds(c * step, step) for c in range(PARTS)]


class Gather:
    def __init__(self, line, ref, sems):
        self.line, self.ref, self.sems = line, ref, sems
        self.rows = part_rows(ref.shape[1])

    def copy(self, side, block, hop, c, peer):
        view = self.ref.at[block, self.rows[c]]
        return pltpu.make_async_remote_copy(
            src_ref=view, dst_ref=view,
            send_sem=self.sems.at[0, side, hop, c], recv_sem=self.sems.at[1, side, hop, c],
            device_id=self.line.peer(peer), device_id_type=MESH,
        )

    def start(self):
        for side in range(2):
            @pl.when(self.line.has(side))
            def _():
                for c in range(PARTS):
                    self.copy(side, self.line.p, 0, c, side).start()

    def arrive(self, block):
        side, hop = self.line.toward(block)
        side = 1 - side
        for c in range(PARTS):
            self.copy(side, block, hop, c, 1 - side).wait_recv()

            @pl.when(self.line.has(side))
            def _():
                self.copy(side, block, hop + 1, c, side).start()

    def hops(self, i):
        return jnp.abs(self.line.arrival(i) - self.line.p)

    def arrive_at(self, i):
        fresh = True if i == 1 else self.hops(i) != self.hops(i - 1)

        @pl.when(fresh)
        def _():
            self.arrive(self.line.arrival(i))

        if i + 1 < self.line.n:
            @pl.when(self.hops(i) == self.hops(i + 1))
            def _():
                self.arrive(self.line.arrival(i + 1))

    def done(self):
        for i in range(self.line.n):
            block = self.line.arrival(i)
            if i == 0:
                for side in range(2):
                    @pl.when(self.line.has(side))
                    def _():
                        for c in range(PARTS):
                            self.copy(side, block, 0, c, side).wait_send()
            else:
                side, hop = self.line.toward(block)
                side = 1 - side

                @pl.when(self.line.has(side))
                def _():
                    for c in range(PARTS):
                        self.copy(side, block, hop + 1, c, side).wait_send()


class Reduce:
    def __init__(self, line, held, out, box, sems):
        self.line, self.held, self.out, self.box, self.sems = line, held, out, box, sems
        self.rows = part_rows(out.shape[2])

    def copy(self, side, slot, c, peer):
        return pltpu.make_async_remote_copy(
            src_ref=self.out.at[side, slot, self.rows[c]],
            dst_ref=self.box.at[side, slot, self.rows[c]],
            send_sem=self.sems.at[0, side, slot, c], recv_sem=self.sems.at[1, side, slot, c],
            device_id=self.line.peer(peer), device_id_type=MESH,
        )

    def free(self, d):
        return jnp.logical_not(self.line.fed(self.line.toward(d)[0]))

    def emit(self, d):
        side, slot = self.line.toward(d)
        for c in range(PARTS):
            rows = self.rows[c]

            @pl.when(self.line.fed(side))
            def _():
                self.copy(side, slot + 1, c, 1 - side).wait_recv()
                self.held[d, rows] = self.held[d, rows] + self.box[side, slot + 1, rows].astype(F32)

            self.out[side, slot, rows] = self.held[d, rows].astype(BF16)
            self.copy(side, slot, c, side).start()

    def finish(self):
        for side in range(2):
            @pl.when(self.line.fed(side))
            def _():
                for c in range(PARTS):
                    self.copy(side, 0, c, 1 - side).wait_recv()
                self.held[self.line.p] = self.held[self.line.p] + self.box[side, 0].astype(F32)

    def done(self):
        for i in range(1, self.line.n):
            side, slot = self.line.toward(self.line.early(i))
            for c in range(PARTS):
                self.copy(side, slot, c, side).wait_send()


def fill(target, column, bits, lhs, values):
    width = lhs.shape[1]
    rows = width >> bits
    step = max(rows, 256)
    for base in range(0, width, step):
        value = dot(lhs[:, base : base + step], values, TN).astype(BF16)
        for inner in range(0, step, rows):
            block = (base + inner) // rows
            lead = tuple((block >> b) % 2 for b in range(bits - 1, -1, -1))
            target[lead + (slice(None), slice(column, column + values.shape[1]))] = value[
                inner : inner + rows
            ]


class Scatter:
    def __init__(self, bits, source, result, inbox, total, streams, sems):
        self.bits, self.source, self.result = bits, source, result
        self.inbox, self.total, self.streams, self.sems = inbox, total, streams, sems
        self.dp = lax.axis_index("dp")
        self.copies = []

    def bit(self, b):
        return lax.rem(self.dp // (1 << b), 2)

    def partner(self, b):
        return {"dp": self.dp + (1 - 2 * self.bit(b)) * (1 << b)}

    def targets(self):
        return [self.partner(b) for b in range(self.bits)]

    def send(self, b, src, dst, slot):
        copy = pltpu.make_async_remote_copy(
            src_ref=src, dst_ref=dst, send_sem=self.sems.at[0, slot], recv_sem=self.sems.at[1, slot],
            device_id=self.partner(b), device_id_type=MESH,
        )
        copy.start()
        self.copies.append(copy)
        return copy

    def orders(self):
        rest = list(range(1, self.bits))
        return rest, rest[::-1]

    def step(self, phase):
        if phase == 0:
            lead = (slice(None),) * (self.bits - 1)
            self.waiting = [self.send(0, self.source.at[lead + (1 - self.bit(0),)], self.inbox, 0)]
            return
        if phase == 1:
            lead = (slice(None),) * (self.bits - 1)
            self.waiting[0].wait_recv()
            self.total[...] = (
                self.source[lead + (self.bit(0),)].astype(F32) + self.inbox[...].astype(F32)
            ).astype(BF16)
            self.held = [(self.total, list(range(self.bits - 1, 0, -1)))] * 2
        waiting = []
        for s, order in enumerate(self.orders()):
            low, high, sums, boxes = self.streams[s]
            if phase > 1:
                b = order[phase - 2]
                ref, axes = self.held[s]
                self.waiting[s].wait_recv()
                columns = (slice(None), slice(low, high) if phase == 2 else slice(None))
                lead = tuple(self.bit(b) if a == b else slice(None) for a in axes)
                value = ref[lead + columns].astype(F32) + boxes[phase - 2][...].astype(F32)
                if phase == self.bits:
                    self.result[:, low:high] = value
                else:
                    sums[phase - 2][...] = value.astype(BF16)
                    self.held[s] = (sums[phase - 2], [a for a in axes if a != b])
            if phase < self.bits:
                b = order[phase - 1]
                ref, axes = self.held[s]
                columns = (slice(None), slice(low, high) if phase == 1 else slice(None))
                lead = tuple(1 - self.bit(b) if a == b else slice(None) for a in axes)
                slot = 1 + s * (self.bits - 1) + phase - 1
                waiting.append(self.send(b, ref.at[lead + columns], boxes[phase - 1], slot))
        self.waiting = waiting

    def finish(self):
        for copy in self.copies:
            copy.wait_send()


def scatter_scratch(bits, rows, width):
    middle = width // (2 * LANES) * LANES
    shapes = [
        pltpu.VMEM((rows, width), F32),
        pltpu.VMEM((2,) * (bits - 1) + (rows, width), BF16),
        pltpu.VMEM((2,) * (bits - 1) + (rows, width), BF16),
    ]
    for low, high in ((0, middle), (middle, width)):
        for kind in range(2):
            for left in range(bits - 2, -1, -1):
                shapes.append(pltpu.VMEM((2,) * left + (rows, high - low), BF16))
    shapes.append(pltpu.SemaphoreType.DMA((2, 2 * bits - 1)))
    return shapes


def scatter_of(bits, source, scratch):
    result, inbox, total = scratch[:3]
    width = result.shape[1]
    middle = width // (2 * LANES) * LANES
    each = bits - 1
    refs = scratch[3:-1]
    streams = []
    for s, (low, high) in enumerate(((0, middle), (middle, width))):
        part = refs[2 * each * s : 2 * each * (s + 1)]
        streams.append((low, high, part[:each], part[each:]))
    return Scatter(bits, source, result, inbox, total, streams, scratch[-1])


def narrow_parts(wd_ref, wb_ref, heads, wdb_ref):
    wdb_ref[...] = jnp.zeros_like(wdb_ref)
    wdb_ref[0:heads, :] = wd_ref[...].astype(F32)
    wdb_ref[heads : 2 * heads, :] = wb_ref[...].astype(F32)


def project_kernel(
    n, heads, dk, dv,
    x_ref, grad_ref, gain_ref, wq_ref, wk_ref, wv_ref, wg_ref, wd_ref, wb_ref, *rest
):
    consts = rest[:6]
    xn_ref, gfull_ref, q_ref, k_ref, v_ref, gate_ref, db_ref = rest[6:13]
    outs = rest[13:18]
    scratch = rest[18:22]
    xsems, gsems, wdb_ref, rate_ref = rest[22:]
    narrow_parts(wd_ref, wb_ref, heads, wdb_ref)
    rate_ref[...] = jnp.zeros_like(rate_ref)
    rate_ref[:, :heads] = consts[4][...]
    consts = consts[:4] + (rate_ref,) + consts[5:]
    ring = Ring(n)
    count = x_ref.shape[0]
    x = x_ref[...].astype(F32)
    rate = lax.rsqrt(jnp.mean(x * x, axis=-1, keepdims=True) + EPS_NORM)
    xn_ref[ring.me] = (x * rate * gain_ref[...]).astype(BF16)
    gfull_ref[ring.me] = grad_ref[...]
    enter(ring.targets())
    line = Line(n)
    gather = Gather(line, xn_ref, xsems)
    share = Gather(line, gfull_ref, gsems)
    gather.start()

    def project(index):
        rows = rows_of(index, count)
        chunk = xn_ref[index]
        for w, out in ((wq_ref, q_ref), (wk_ref, k_ref), (wv_ref, v_ref), (wg_ref, gate_ref)):
            out[rows, :] = dot(chunk, w[...])
        db_ref[rows, :] = dot(chunk, wdb_ref[...], NT)

    project(line.p)
    for i in range(1, n):
        gather.arrive_at(i)
        if i == n - 1:
            share.start()
        project(line.arrival(i))

    mixer_forward_kernel(
        heads, dk, dv, q_ref, k_ref, v_ref, gate_ref, db_ref, *consts, *outs, *scratch,
        tick=lambda i: share.arrive_at(i) if i < n else None,
    )
    for i in range(3, n):
        share.arrive_at(i)
    gather.done()
    share.done()


def project_mix(n, heads, x, grad, gain, wq, wk, wv, wg, wd, wb, *consts):
    count, width = x.shape
    length = count * n
    dk, dv = wq.shape[1] // heads, wv.shape[1] // heads
    pairs = heads * (length // GROUP)
    f32 = lambda *shape: jax.ShapeDtypeStruct(shape, F32)
    shapes = (
        jax.ShapeDtypeStruct((n, count, width), BF16),
        jax.ShapeDtypeStruct((n, count, width), BF16),
        f32(length, heads * dk), f32(length, heads * dk), f32(length, heads * dv),
        f32(length, heads * dv), f32(length, LANES),
        jax.ShapeDtypeStruct((length, heads * dv), BF16),
        f32(pairs, GROUP, GROUP), f32(length, heads * dv), f32(pairs, dk, dv),
        f32(length, heads * dv),
    )
    dma = pltpu.SemaphoreType.DMA((2, 2, n - 1, PARTS))
    return pl.pallas_call(
        partial(project_kernel, n, heads, dk, dv),
        out_shape=shapes,
        in_specs=vmem_specs(15),
        out_specs=tuple(vmem_specs(12)),
        scratch_shapes=[
            pltpu.VMEM((length, heads * dk), F32), pltpu.VMEM((length, heads * dk), F32),
            pltpu.VMEM((length, heads * dv), F32), pltpu.VMEM((heads, dk, dv), F32),
            dma, dma, pltpu.VMEM((LANES, width), F32), pltpu.VMEM((1, LANES), F32),
        ],
        compiler_params=pltpu.CompilerParams(
            collective_id=0, has_side_effects=True, vmem_limit_bytes=VMEM_BYTES
        ),
        name="project_mix",
    )(x, grad, gain, wq, wk, wv, wg, wd, wb, *consts)


def middle_kernel(
    n, bits,
    gated_ref, x_ref, grad_ref, gfull_ref, wout_ref, gain_ref, wfg_ref, wfu_ref, wfd_ref,
    resid_ref, dresid_ref, ffn_ref, dgated_ref, gout_ref, first_ref, gfgain_ref,
    out_send, out_box, hn, dh_send, dh_box, dres, d_act, act, d_in, d_val, held, grads, sems,
    *scratch
):
    ring = Ring(n)
    count, width = x_ref.shape
    columns = wfg_ref.shape[0]
    padded = columns + (-columns % LANES)
    enter(ring.targets() + scatter_of(bits, grads, scratch).targets())
    flat = lambda ref: ref[...].reshape(n * count, ref.shape[2])
    if padded > columns:
        for i in range(3):
            tail = slice((i + 1) * padded - LANES, (i + 1) * padded)
            grads[(slice(None),) * (bits + 1) + (tail,)] = jnp.zeros(
                grads.shape[:-1] + (LANES,), BF16
            )

    def feed(index):
        chunk = hn[index]
        up_in = dot(chunk, wfg_ref[...], NT)
        up_val = dot(chunk, wfu_ref[...], NT)
        sig = sigmoid(up_in)
        d_chunk = d_act[index]
        half = up_in * sig
        act[index] = (half * up_val).astype(BF16)
        d_in[index] = (d_chunk * up_val * sig * (1.0 + up_in * (1.0 - sig))).astype(BF16)
        d_val[index] = (d_chunk * half).astype(BF16)
        held[index] = dot(d_in[index], wfg_ref[...]) + dot(d_val[index], wfu_ref[...])

    line = Line(n)
    p = line.p
    scatter = scatter_of(bits, grads, scratch)
    part = lambda d: dot(gated_ref[rows_of(d, count), :], wout_ref[...])
    sums = Reduce(line, held, out_send, out_box, sems.at[0])
    for i in range(1, n):
        d = line.early(i)
        held[d] = part(d)
        sums.emit(d)
    held[p] = x_ref[...].astype(F32) + part(p)
    for i in range(n):
        d_act[i] = dot(gfull_ref[i], wfd_ref[...], NT)
    sums.finish()
    resid = held[p]
    resid_ref[...] = resid
    rate = lax.rsqrt(jnp.mean(resid * resid, axis=-1, keepdims=True) + EPS_NORM)
    hn[p] = (resid * rate * gain_ref[...]).astype(BF16)
    share = Gather(line, hn, sems.at[1])
    share.start()
    feed(p)
    back = Reduce(line, held, dh_send, dh_box, sems.at[2])
    for i in range(1, n):
        share.arrive_at(i)
        d = line.arrival(i)
        feed(d)
        pl.when(back.free(d))(partial(back.emit, d))
    for i in range(1, n):
        d = line.late(i)
        pl.when(jnp.logical_not(back.free(d)))(partial(back.emit, d))
    for i, (left, right) in enumerate(((hn, d_in), (hn, d_val), (gfull_ref, act))):
        fill(grads, i * padded, bits, flat(left), flat(right))
    scatter.step(0)
    back.finish()
    d_hnorm = held[p]
    resid = resid_ref[...]
    rate = lax.rsqrt(jnp.mean(resid * resid, axis=-1, keepdims=True) + EPS_NORM)
    plain = resid * rate
    gfgain_ref[...] = jnp.sum(d_hnorm * plain, axis=0, keepdims=True)
    up = d_hnorm * gain_ref[...]
    d_resid = grad_ref[...].astype(F32) + rate * (
        up - plain * jnp.mean(up * plain, axis=-1, keepdims=True)
    )
    dresid_ref[...] = d_resid
    dres[p] = d_resid.astype(BF16)
    spread = Gather(line, dres, sems.at[3])
    spread.start()

    def back_out(d):
        dgated_ref[rows_of(d, count), :] = dot(dres[d], wout_ref[...], NT)

    back_out(p)
    scatter.step(1)
    for i in range(1, n):
        spread.arrive_at(i)
        back_out(line.arrival(i))
        if i == 1:
            for k in range(n):
                ffn_ref[k * count : (k + 1) * count, :] = dot(act[k], wfd_ref[...]).astype(BF16)
        if i == n - 1:
            scatter.step(2)
    lhs = flat(dres)
    step = math.gcd(width, 256)
    for base in range(0, width, step):
        gout_ref[base : base + step, :] = dot(
            lhs[:, base : base + step], gated_ref[...], TN
        ).astype(BF16)
    for phase in range(3, bits + 1):
        scatter.step(phase)
    first_ref[...] = scratch[0][...]
    for group in (sums, share, back, spread):
        group.done()
    scatter.finish()


def middle(n, bits, gated, x, grad, gfull, wout, gain, wfg, wfu, wfd):
    count, width = x.shape
    length = n * count
    inner, columns = wout.shape[0], wfg.shape[0]
    padded = columns + (-columns % LANES)
    rows = width >> bits
    f32 = lambda *shape: jax.ShapeDtypeStruct(shape, F32)
    slots = pltpu.VMEM((2, n - 1, count, width), BF16)
    return pl.pallas_call(
        partial(middle_kernel, n, bits),
        out_shape=(
            f32(count, width), f32(count, width),
            jax.ShapeDtypeStruct((length, width), BF16),
            f32(length, inner),
            jax.ShapeDtypeStruct((width, inner), BF16),
            f32(rows, 3 * padded),
            f32(1, width),
        ),
        in_specs=vmem_specs(9),
        out_specs=tuple(vmem_specs(7)),
        scratch_shapes=[
            slots, slots, pltpu.VMEM((n, count, width), BF16), slots, slots,
            pltpu.VMEM((n, count, width), BF16),
            pltpu.VMEM((n, count, columns), F32),
            pltpu.VMEM((n, count, columns), BF16),
            pltpu.VMEM((n, count, columns), BF16),
            pltpu.VMEM((n, count, columns), BF16),
            pltpu.VMEM((n, count, width), F32),
            pltpu.VMEM((2,) * bits + (rows, 3 * padded), BF16),
            pltpu.SemaphoreType.DMA((4, 2, 2, n - 1, PARTS)),
        ] + scatter_scratch(bits, rows, 3 * padded),
        compiler_params=pltpu.CompilerParams(
            collective_id=1, has_side_effects=True, vmem_limit_bytes=VMEM_BYTES
        ),
        name="middle",
    )(gated, x, grad, gfull, wout, gain, wfg, wfu, wfd)


def back_kernel(n, bits, heads, dk, dv, *refs):
    mixer_in, (gout_ref, xn_ref, ffn_ref, resid_ref) = refs[:16], refs[16:20]
    mixer_out, (block_ref, first_ref) = refs[20:26], refs[26:28]
    mixer_scratch, (boxes, fsems, rate_ref, grads), scratch = refs[28:38], refs[38:42], refs[42:]
    rate_ref[...] = jnp.zeros_like(rate_ref)
    rate_ref[:, :heads] = mixer_in[9][...]
    mixer_in = mixer_in[:9] + (rate_ref,) + mixer_in[10:]
    d_ref = mixer_out[0]
    ring = Ring(n)
    scatter = scatter_of(bits, grads, scratch)
    enter(ring.targets() + scatter.targets())
    inner = gout_ref.shape[1]
    rows = gout_ref.shape[0] >> bits

    def tick(phase):
        if phase == 0:
            for block in range(1 << bits):
                lead = tuple((block >> b) % 2 for b in range(bits - 1, -1, -1))
                grads[lead + (slice(None), slice(0, inner))] = gout_ref[
                    block * rows : (block + 1) * rows
                ]
            lhs = xn_ref[...].reshape(d_ref.shape[0], xn_ref.shape[2])
            base = 2 * heads * (dk + dv) - heads * dv
            fill(grads, inner, bits, lhs, d_ref[:, base : base + heads * dv])
        scatter.step(phase)

    count = resid_ref.shape[0]
    sends = {}
    for k in ring.steps:
        sends[k] = ring.copy(
            k, ffn_ref.at[rows_of(ring.to(k), count), :], boxes.at[k - 1], fsems.at[0], fsems.at[1]
        )
        sends[k].start()
    mixer_backward_kernel(heads, dk, dv, *mixer_in, *mixer_out, *mixer_scratch, tick=tick)
    for phase in range(3, bits + 1):
        scatter.step(phase)
    block = resid_ref[...] + ffn_ref[rows_of(ring.me, count), :].astype(F32)
    for k in ring.steps:
        sends[k].wait_recv()
        block = block + boxes[k - 1].astype(F32)
    block_ref[...] = block.astype(BF16)
    first_ref[...] = scratch[0][...]
    for k in ring.steps:
        sends[k].wait_send()
    scatter.finish()


def backward(n, bits, heads, mixer_in, g_out, xnorm, ffn, resid):
    q, v = mixer_in[0], mixer_in[2]
    length = q.shape[0]
    dk, dv = q.shape[1] // heads, v.shape[1] // heads
    wide_out = 2 * heads * dk + 2 * heads * dv + LANES
    count, width = resid.shape
    rows = width >> bits
    second = g_out.shape[1] + heads * dv
    f32 = lambda *shape: jax.ShapeDtypeStruct(shape, F32)
    shapes = (
        jax.ShapeDtypeStruct((length, wide_out), BF16),
        f32(*mixer_in[6].shape), f32(*mixer_in[7].shape), f32(*mixer_in[8].shape),
        f32(1, LANES), f32(1, dv),
        jax.ShapeDtypeStruct((count, width), BF16),
        f32(rows, second),
    )
    narrow, broad = (length, heads * dk), (length, heads * dv)
    return pl.pallas_call(
        partial(back_kernel, n, bits, heads, dk, dv),
        out_shape=shapes,
        in_specs=vmem_specs(20),
        out_specs=tuple(vmem_specs(8)),
        scratch_shapes=[
            pltpu.VMEM(narrow, F32), pltpu.VMEM(narrow, F32), pltpu.VMEM(broad, F32),
            pltpu.VMEM(broad, F32), pltpu.VMEM(narrow, F32), pltpu.VMEM(narrow, F32),
            pltpu.VMEM(broad, F32), pltpu.VMEM((heads, dk, dv), F32),
            pltpu.VMEM((length, LANES), F32), pltpu.VMEM((length, LANES), F32),
            pltpu.VMEM((n - 1, count, width), BF16), pltpu.SemaphoreType.DMA((2, n - 1)),
            pltpu.VMEM((1, LANES), F32),
            pltpu.VMEM((2,) * bits + (rows, second), BF16),
        ] + scatter_scratch(bits, rows, second),
        compiler_params=pltpu.CompilerParams(
            collective_id=2, has_side_effects=True, vmem_limit_bytes=VMEM_BYTES
        ),
        name="mixer_back",
    )(*mixer_in, g_out, xnorm, ffn, resid)


def last_kernel(n, bits, heads, dk, dv, *refs):
    (d_ref, xn_ref, x_ref, gain_ref, dresid_ref, wq_ref, wk_ref, wv_ref, wg_ref, wd_ref, wb_ref,
     gq_ref, gk_ref, gv_ref, grate_ref, gogain_ref, gfgain_ref) = refs[:17]
    dx_ref, rest_ref, final_ref = refs[17:20]
    grads, dx_send, dx_box, gains, small, small_in, sems, dx_sems, small_sems, wdb_ref, held = (
        refs[20:31]
    )
    scratch = refs[31:]
    narrow_parts(wd_ref, wb_ref, heads, wdb_ref)
    ring = Ring(n)
    scatter = scatter_of(bits, grads, scratch)
    enter(ring.targets() + scatter.targets())
    count, width = x_ref.shape
    weights = (wq_ref, wk_ref, wv_ref, wg_ref)
    span = gains.shape[2]
    line = Line(n)
    p = line.p
    sums = Reduce(line, held, dx_send, dx_box, dx_sems)
    g_again = jnp.zeros((1, width), F32)
    for i in list(range(1, n)) + [0]:
        d = line.early(i)
        rows = rows_of(d, count)
        base, total = 0, None
        for w in weights:
            part = dot(d_ref[rows, base : base + w.shape[1]], w[...], NT)
            total = part if total is None else total + part
            base += w.shape[1]
        total = total + dot(d_ref[rows, base:], wdb_ref[...])
        held[d] = total
        g_again = g_again + jnp.sum(total * xn_ref[d].astype(F32), axis=0, keepdims=True)
        if i > 0:
            pl.when(sums.free(d))(partial(sums.emit, d))
    gains[p] = jnp.zeros((8, span), F32)
    gains[p, 0:1, :width] = g_again / gain_ref[...]
    gains[p, 1:2, :width] = gfgain_ref[...]
    gains[p, 2:3, :dv] = gogain_ref[...]
    shares = ring.share(gains, sems.at[0], sems.at[1])
    lhs = xn_ref[...].reshape(n * count, width)
    front = 2 * heads * dk + heads * dv
    fill(grads, 0, bits, lhs, d_ref[:, :front])
    fill(grads, front, bits, lhs, d_ref[:, front + heads * dv :])
    scatter.step(0)
    for i in range(1, n):
        d = line.early(i)
        pl.when(jnp.logical_not(sums.free(d)))(partial(sums.emit, d))
    small[0] = jnp.zeros(small.shape[1:], F32)
    narrow, broad = heads * dk, heads * dv
    taps = gq_ref.shape[0]
    small[0, 0:taps, :narrow] = gq_ref[...]
    small[0, 0:taps, narrow : 2 * narrow] = gk_ref[...]
    small[0, 0:taps, 2 * narrow : 2 * narrow + broad] = gv_ref[...]
    small[0, 8:9, :LANES] = grate_ref[...]
    for k in ring.steps:
        shares[k].wait_recv()
    total = gains[0]
    for i in range(1, n):
        total = total + gains[i]
    small[0, 16:24, :] = total
    swaps = []

    def swap(b):
        copy = pltpu.make_async_remote_copy(
            src_ref=small.at[b], dst_ref=small_in.at[b],
            send_sem=small_sems.at[0, b], recv_sem=small_sems.at[1, b],
            device_id=scatter.partner(b), device_id_type=MESH,
        )
        copy.start()
        swaps.append(copy)

    for b in range(bits):
        swap(b)
        scatter.step(b + 1)
        swaps[b].wait_recv()
        small[b + 1] = small[b] + small_in[b]
    final_ref[...] = small[bits]
    rest_ref[...] = scratch[0][...]
    sums.finish()
    d_xnorm = held[p]
    x = x_ref[...].astype(F32)
    rate = lax.rsqrt(jnp.mean(x * x, axis=-1, keepdims=True) + EPS_NORM)
    plain = x * rate
    up = d_xnorm * gain_ref[...]
    dx_ref[...] = (
        dresid_ref[...] + rate * (up - plain * jnp.mean(up * plain, axis=-1, keepdims=True))
    ).astype(BF16)
    sums.done()
    for k in ring.steps:
        shares[k].wait_send()
    for copy in swaps:
        copy.wait_send()
    scatter.finish()


def last(n, bits, heads, *args):
    d_cat, xn, x, _, _, wq, _, wv = args[:8]
    narrow, broad = wq.shape[1], wv.shape[1]
    dk, dv = narrow // heads, broad // heads
    count, width = x.shape
    rows = width >> bits
    span = max(width, 2 * narrow + broad)
    f32 = lambda *shape: jax.ShapeDtypeStruct(shape, F32)
    slots = pltpu.VMEM((2, n - 1, count, width), BF16)
    cut = d_cat.shape[1] - broad
    return pl.pallas_call(
        partial(last_kernel, n, bits, heads, dk, dv),
        out_shape=(
            jax.ShapeDtypeStruct((count, width), BF16),
            f32(rows, cut), f32(24, span),
        ),
        in_specs=vmem_specs(17),
        out_specs=tuple(vmem_specs(3)),
        scratch_shapes=[
            pltpu.VMEM((2,) * bits + (rows, cut), BF16),
            slots, slots,
            pltpu.VMEM((n, 8, span), F32),
            pltpu.VMEM((bits + 1, 24, span), F32),
            pltpu.VMEM((bits, 24, span), F32),
            pltpu.SemaphoreType.DMA((2, n - 1)),
            pltpu.SemaphoreType.DMA((2, 2, n - 1, PARTS)),
            pltpu.SemaphoreType.DMA((2, bits)),
            pltpu.VMEM((LANES, width), F32),
            pltpu.VMEM((n, count, width), F32),
        ] + scatter_scratch(bits, rows, cut),
        compiler_params=pltpu.CompilerParams(
            collective_id=3, has_side_effects=True, vmem_limit_bytes=VMEM_BYTES
        ),
        name="last",
    )(*args)


def finish_kernel(heads, dk, dv, columns, taps, *refs):
    block_in, dx_in, first, second, rest, small = refs[:6]
    (block, dx, again, sq, sk, sv, sg, sd, sb, cq, ck, cv, rate, ogain, sout, fgain,
     sgate, sup, sdown) = refs[6:]
    block[...] = block_in[...]
    dx[...] = dx_in[...]
    narrow, broad = heads * dk, heads * dv
    width = again.shape[1]
    sq[...] = rest[:, :narrow]
    sk[...] = rest[:, narrow : 2 * narrow]
    base = 2 * narrow
    sv[...] = rest[:, base : base + broad]
    inner = sout.shape[0]
    sg[...] = second[:, inner:]
    tail = rest[:, base + broad :].T
    sd[...] = tail[0:heads]
    sb[...] = tail[heads : 2 * heads]
    cq[...] = small[0:taps, :narrow]
    ck[...] = small[0:taps, narrow : 2 * narrow]
    cv[...] = small[0:taps, 2 * narrow : 2 * narrow + broad]
    rate[...] = small[8:9, :heads]
    again[...] = small[16:17, :width]
    fgain[...] = small[17:18, :width]
    ogain[...] = small[18:19, :dv]
    padded = columns + (-columns % LANES)
    sgate[...] = first[:, :padded].T[:columns]
    sup[...] = first[:, padded : 2 * padded].T[:columns]
    sdown[...] = first[:, 2 * padded : 3 * padded].T[:columns]
    sout[...] = second[:, :inner].T


def finish(heads, dk, dv, columns, taps, block, dx, first, second, rest, small):
    rows, width = rest.shape[0], block.shape[1]
    narrow, broad = heads * dk, heads * dv
    inner = second.shape[1] - broad
    f32 = lambda *shape: jax.ShapeDtypeStruct(shape, F32)
    return pl.pallas_call(
        partial(finish_kernel, heads, dk, dv, columns, taps),
        out_shape=(
            jax.ShapeDtypeStruct(block.shape, BF16), jax.ShapeDtypeStruct(dx.shape, BF16),
            f32(1, width), f32(rows, narrow), f32(rows, narrow), f32(rows, broad),
            f32(rows, broad), f32(heads, rows), f32(heads, rows), f32(taps, narrow),
            f32(taps, narrow), f32(taps, broad), f32(1, heads), f32(1, dv), f32(inner, rows),
            f32(1, width), f32(columns, rows), f32(columns, rows), f32(columns, rows),
        ),
        in_specs=vmem_specs(6),
        out_specs=tuple(vmem_specs(19)),
        compiler_params=pltpu.CompilerParams(vmem_limit_bytes=24 << 20),
        name="finish",
    )(block, dx, first, second, rest, small)


def body(
    n,
    bits,
    tokens,
    seg_ids,
    attn_gain,
    w_query,
    w_key,
    w_value,
    w_gate,
    w_decay,
    w_beta,
    conv_query,
    conv_key,
    conv_value,
    decay_rate,
    out_gain,
    w_out,
    ffn_gain,
    w_ffn_gate,
    w_ffn_up,
    w_ffn_down,
    grad_out,
):
    heads = w_decay.shape[1]
    row = lambda array: array.reshape(1, -1)
    columns = w_ffn_gate.shape[1]
    taps = conv_query.shape[0]
    dk, dv = w_query.shape[1] // heads, w_value.shape[1] // heads
    consts = (seg_ids, conv_query, conv_key, conv_value, row(decay_rate), row(out_gain))
    xnorm, grad_full, *projs, gated, inv, delta, states, mixed = project_mix(
        n, heads, tokens, grad_out, row(attn_gain), w_query, w_key, w_value, w_gate,
        w_decay.T, w_beta.T, *consts
    )
    resid, d_resid, ffn, d_gated, g_out, first, g_fgain = middle(
        n, bits, gated, tokens, grad_out, grad_full, w_out, row(ffn_gain),
        w_ffn_gate.T, w_ffn_up.T, w_ffn_down
    )
    mixer_in = (*projs, *consts, inv, delta, states, mixed, d_gated)
    d_cat, g_cq, g_ck, g_cv, g_rate, g_ogain, block_out, second = backward(
        n, bits, heads, mixer_in, g_out, xnorm, ffn, resid
    )
    grad_tokens, rest, small = last(
        n, bits, heads, d_cat, xnorm, tokens, row(attn_gain), d_resid, w_query, w_key, w_value,
        w_gate, w_decay.T, w_beta.T, g_cq, g_ck, g_cv, g_rate, g_ogain, g_fgain
    )
    (block_out, grad_tokens, again, s_query, s_key, s_value, s_gate, s_decay, s_beta, cq, ck, cv,
     rate, ogain, s_out, fgain, s_fgate, s_fup, s_down) = finish(
        heads, dk, dv, columns, taps, block_out, grad_tokens, first, second, rest, small
    )
    flat = lambda array: array.reshape(-1)
    return (
        block_out, grad_tokens, flat(again), s_query, s_key, s_value, s_gate, s_decay.T, s_beta.T,
        cq, ck, cv, flat(rate), flat(ogain), s_out, flat(fgain), s_fgate.T, s_fup.T, s_down,
    )


def solution(mesh):
    in_specs = (
        P(("dp", "tensor"), None),
        P("dp", None),
        P(),
        P(None, "tensor"),
        P(None, "tensor"),
        P(None, "tensor"),
        P(None, "tensor"),
        P(None, "tensor"),
        P(None, "tensor"),
        P(None, "tensor"),
        P(None, "tensor"),
        P(None, "tensor"),
        P("tensor"),
        P(),
        P("tensor", None),
        P(),
        P(None, "tensor"),
        P(None, "tensor"),
        P("tensor", None),
        P(("dp", "tensor"), None),
    )
    out_specs = (
        P(("dp", "tensor"), None),
        P(("dp", "tensor"), None),
        P(),
        P("dp", "tensor"),
        P("dp", "tensor"),
        P("dp", "tensor"),
        P("dp", "tensor"),
        P("dp", "tensor"),
        P("dp", "tensor"),
        P(None, "tensor"),
        P(None, "tensor"),
        P(None, "tensor"),
        P("tensor"),
        P(),
        P("tensor", "dp"),
        P(),
        P("dp", "tensor"),
        P("dp", "tensor"),
        P("tensor", "dp"),
    )
    n = mesh.shape["tensor"]
    bits = mesh.shape["dp"].bit_length() - 1
    return jax.shard_map(partial(body, n, bits), mesh=mesh, in_specs=in_specs, out_specs=out_specs, check_vma=False)
```

```python
from functools import partial
import math

import jax
import jax.numpy as jnp
from jax import lax
from jax.experimental import pallas as pl
from jax.experimental.pallas import tpu as pltpu
from jax.sharding import PartitionSpec as P

GROUP = 64
LANES = 128
EPS_NORM = 1e-05
EPS_UNIT = 1e-06
HIGHEST = lax.Precision.HIGHEST
HIGH = lax.Precision.HIGH
F32 = jnp.float32
BF16 = jnp.bfloat16
MESH = pl.DeviceIdType.MESH
NN = (((1,), (0,)), ((), ()))
NT = (((1,), (1,)), ((), ()))
TN = (((0,), (0,)), ((), ()))
PROJECT_BYTES = 28 << 20
MIDDLE_BYTES = 46 << 20
BACK_BYTES = 36 << 20
LAST_BYTES = 28 << 20


def dot(a, b, dims=NN):
    return lax.dot_general(a.astype(BF16), b.astype(BF16), dims, preferred_element_type=F32)


def dot_fine(a, b, dims=NN):
    return lax.dot_general(a, b, dims, precision=HIGH, preferred_element_type=F32)


def shift_down(values, offset, keep):
    return pltpu.roll(values, offset, 0) * keep


def shift_up(values, offset, keep):
    rolled = values * keep
    return pltpu.roll(rolled, values.shape[0] - offset, 0)


def spread_lanes(seg_row):
    return jnp.broadcast_to(seg_row, (LANES, seg_row.shape[1])).T


def conv_keeps(seg, taps):
    length = seg.shape[0]
    row = lax.broadcasted_iota(jnp.int32, (length, LANES), 0)
    keeps = []
    for offset in range(1, taps):
        same = (seg == pltpu.roll(seg, offset, 0)) & (row >= offset)
        keeps.append(same.astype(F32))
    return keeps


def wide(keep, columns):
    return jnp.concatenate([keep] * (columns // LANES), axis=1) if columns > LANES else keep


def conv(values, taps, keeps):
    total = taps[0:1] * values
    for offset in range(1, taps.shape[0]):
        total = total + taps[offset : offset + 1] * shift_down(
            values, offset, wide(keeps[offset - 1], values.shape[1])
        )
    return total


def conv_back(values, taps, keeps, d_out):
    d_values = taps[0:1] * d_out
    d_taps = [jnp.sum(values * d_out, axis=0, keepdims=True)]
    for offset in range(1, taps.shape[0]):
        keep = wide(keeps[offset - 1], values.shape[1])
        moved = shift_up(d_out, offset, keep)
        d_values = d_values + taps[offset : offset + 1] * moved
        d_taps.append(jnp.sum(values * moved, axis=0, keepdims=True))
    return d_values, jnp.concatenate(d_taps, axis=0)


def softplus(values):
    return jnp.maximum(values, 0.0) + jnp.log1p(jnp.exp(-jnp.abs(values)))


def sigmoid(values):
    return jax.nn.sigmoid(values)


def silu_back(values):
    sig = sigmoid(values)
    return sig * (1.0 + values * (1.0 - sig))


def block_cumsum(values):
    length = values.shape[0]
    row = lax.broadcasted_iota(jnp.int32, values.shape, 0) % GROUP
    step = 1
    while step < GROUP:
        values = values + jnp.where(row >= step, pltpu.roll(values, step, 0), 0.0)
        step *= 2
    return values


def block_cumsum_back(values):
    length = values.shape[0]
    row = lax.broadcasted_iota(jnp.int32, values.shape, 0) % GROUP
    step = 1
    while step < GROUP:
        values = values + jnp.where(
            row < GROUP - step, pltpu.roll(values, length - step, 0), 0.0
        )
        step *= 2
    return values


def invert(lowers):
    size = lowers[0].shape[0]
    rows = lax.broadcasted_iota(jnp.int32, (size, size), 0)
    cols = lax.broadcasted_iota(jnp.int32, (size, size), 1)
    eye = (rows == cols).astype(F32)
    pair = (rows // 2 == cols // 2).astype(F32)
    done = [eye - low * pair for low in lowers]
    half = 2
    while half < size:
        keep = (rows // (2 * half) == cols // (2 * half)) & (rows // half != cols // half)
        keep = keep.astype(F32)
        steps = [dot_fine(low * keep, inv) for low, inv in zip(lowers, done)]
        done = [inv - dot_fine(inv, step) for inv, step in zip(done, steps)]
        half *= 2
    return done


def block_masks(seg_col, seg_row, cum, cum_t, n, h):
    rows = slice(n * GROUP, (n + 1) * GROUP)
    index_t = lax.broadcasted_iota(jnp.int32, (GROUP, GROUP), 0)
    index_i = lax.broadcasted_iota(jnp.int32, (GROUP, GROUP), 1)
    doc_col = seg_col[rows]
    doc_row = seg_row[:, rows]
    c_col = cum[rows, h : h + 1]
    c_row = cum_t[h : h + 1, rows]
    c_last = c_col[GROUP - 1 : GROUP]
    same = ((doc_col == doc_row) & (index_t >= index_i)).astype(F32)
    spread = jnp.exp(jnp.minimum(c_col - c_row, 0.0)) * same
    strict = (index_t > index_i).astype(F32)
    end_doc = doc_col[GROUP - 1 : GROUP]
    late = jnp.exp(jnp.minimum(c_last - c_col, 0.0)) * (doc_col == end_doc).astype(F32)
    if n == 0:
        carried = jnp.zeros_like(c_col)
    else:
        prev = seg_col[n * GROUP - 1 : n * GROUP]
        carried = jnp.exp(c_col) * (doc_col == prev).astype(F32)
    return spread, strict, late, carried


def unit(values):
    rate = lax.rsqrt(jnp.sum(values * values, axis=-1, keepdims=True) + EPS_UNIT)
    return values * rate, rate


def mixer_forward_kernel(
    heads, dk, dv,
    q_ref, k_ref, v_ref, gate_ref, db_ref, seg_row_ref,
    tq_ref, tk_ref, tv_ref, rate_ref, ogain_ref,
    gated_ref, inv_ref, delta_ref, state_ref, mixed_ref,
    query, keys, values, carry, tick=None,
):
    length = q_ref.shape[0]
    blocks = length // GROUP
    seg_row = seg_row_ref[...].astype(F32)
    seg_wide = spread_lanes(seg_row)
    seg_col = seg_wide[:, :1]
    keeps = conv_keeps(seg_wide, tq_ref.shape[0])
    db = db_ref[...]
    beta = sigmoid(db)
    cum = block_cumsum(-rate_ref[...] * softplus(db))
    cum_t = cum.T
    scale = 1.0 / math.sqrt(dk)
    for h in range(heads):
        cols = slice(h * dk, (h + 1) * dk)
        query[:, cols] = unit(jax.nn.silu(conv(q_ref[:, cols], tq_ref[:, cols], keeps)))[0] * scale
        keys[:, cols] = unit(jax.nn.silu(conv(k_ref[:, cols], tk_ref[:, cols], keeps)))[0]
        cols = slice(h * dv, (h + 1) * dv)
        values[:, cols] = jax.nn.silu(conv(v_ref[:, cols], tv_ref[:, cols], keeps))

    tick(1)
    lowers = []
    for n in range(blocks):
        rows = slice(n * GROUP, (n + 1) * GROUP)
        for h in range(heads):
            key = keys[rows, h * dk : (h + 1) * dk]
            spread, strict, late, carried = block_masks(seg_col, seg_row, cum, cum_t, n, h)
            b = beta[rows, heads + h : heads + h + 1]
            lowers.append(b * dot_fine(key, key, NT) * spread * strict)
    for i, inv in enumerate(invert(lowers)):
        inv_ref[i] = inv
    tick(2)

    for h in range(heads):
        carry[h] = jnp.zeros((dk, dv), F32)
    for n in range(blocks):
        rows = slice(n * GROUP, (n + 1) * GROUP)
        for h in range(heads):
            pair = n * heads + h
            kc, vc = slice(h * dk, (h + 1) * dk), slice(h * dv, (h + 1) * dv)
            key, q, v = keys[rows, kc], query[rows, kc], values[rows, vc]
            spread, strict, late, carried = block_masks(seg_col, seg_row, cum, cum_t, n, h)
            b = beta[rows, heads + h : heads + h + 1]
            inv = inv_ref[pair]
            fresh = dot(inv, b * v)
            state = carry[h]
            state_ref[pair] = state
            if n == 0:
                delta = fresh
            else:
                delta = fresh - dot(dot(inv, (b * carried) * key), state)
            delta_ref[rows, vc] = delta
            mixed = dot(dot(q, key, NT) * spread, delta)
            if n > 0:
                mixed = mixed + dot(q * carried, state)
            mixed_ref[rows, vc] = mixed
            if n < blocks - 1:
                new = dot(key * late, delta, TN)
                if n > 0:
                    new = new + carried[GROUP - 1 : GROUP] * state
                carry[h] = new
    for h in range(heads):
        vc = slice(h * dv, (h + 1) * dv)
        mixed = mixed_ref[:, vc]
        rate = lax.rsqrt(jnp.mean(mixed * mixed, axis=-1, keepdims=True) + EPS_NORM)
        gated_ref[:, vc] = (mixed * rate * ogain_ref[...] * jax.nn.silu(gate_ref[:, vc])).astype(BF16)


def vmem_specs(count):
    return [pl.BlockSpec(memory_space=pltpu.VMEM)] * count


def mixer_backward_kernel(
    heads, dk, dv,
    q_ref, k_ref, v_ref, gate_ref, db_ref, seg_row_ref,
    tq_ref, tk_ref, tv_ref, rate_ref, ogain_ref,
    inv_ref, delta_ref, state_ref, mixed_ref, dgated_ref,
    d_ref, gq_ref, gk_ref, gv_ref, grate_ref, gogain_ref,
    keys, query, values, d_mixed, d_key, d_query, d_value, d_carry, d_cum, d_beta,
    tick=None,
):
    length = q_ref.shape[0]
    blocks = length // GROUP
    seg_row = seg_row_ref[...].astype(F32)
    seg_wide = spread_lanes(seg_row)
    seg_col = seg_wide[:, :1]
    keeps = conv_keeps(seg_wide, tq_ref.shape[0])
    db = db_ref[...]
    beta = sigmoid(db)
    rate_row = rate_ref[...]
    soft = softplus(db)
    cum = block_cumsum(-rate_row * soft)
    cum_t = cum.T
    scale = 1.0 / math.sqrt(dk)
    v_base = 2 * heads * dk
    g_base = v_base + heads * dv
    b_base = g_base + heads * dv

    g_ogain = jnp.zeros((1, dv), F32)
    for h in range(heads):
        vc = slice(h * dv, (h + 1) * dv)
        mixed = mixed_ref[:, vc]
        gate = gate_ref[:, vc]
        dg = dgated_ref[:, vc]
        rate = lax.rsqrt(jnp.mean(mixed * mixed, axis=-1, keepdims=True) + EPS_NORM)
        plain = mixed * rate
        sig = sigmoid(gate)
        d_norm = dg * gate * sig
        d_ref[:, g_base + h * dv : g_base + (h + 1) * dv] = (
            dg * plain * ogain_ref[...] * sig * (1.0 + gate * (1.0 - sig))
        ).astype(BF16)
        g_ogain = g_ogain + jnp.sum(d_norm * plain, axis=0, keepdims=True)
        up = d_norm * ogain_ref[...]
        d_mixed[:, vc] = rate * (up - plain * jnp.mean(up * plain, axis=-1, keepdims=True))
        kc = slice(h * dk, (h + 1) * dk)
        query[:, kc] = unit(jax.nn.silu(conv(q_ref[:, kc], tq_ref[:, kc], keeps)))[0] * scale
        keys[:, kc] = unit(jax.nn.silu(conv(k_ref[:, kc], tk_ref[:, kc], keeps)))[0]
        values[:, vc] = jax.nn.silu(conv(v_ref[:, vc], tv_ref[:, vc], keeps))
        d_carry[h] = jnp.zeros((dk, dv), F32)
    gogain_ref[...] = g_ogain
    tick(0)

    lane = lax.broadcasted_iota(jnp.int32, (GROUP, LANES), 1)
    row_col = lax.broadcasted_iota(jnp.int32, (GROUP, 1), 0)
    index_t = lax.broadcasted_iota(jnp.int32, (GROUP, GROUP), 0)
    index_i = lax.broadcasted_iota(jnp.int32, (GROUP, GROUP), 1)
    eye = (index_t == index_i).astype(F32)
    for n in reversed(range(blocks)):
        if n == blocks // 2 - 1:
            tick(1)
        rows = slice(n * GROUP, (n + 1) * GROUP)
        dc_block = jnp.zeros((GROUP, LANES), F32)
        db_block = jnp.zeros((GROUP, LANES), F32)
        last = n == blocks - 1
        for h in range(heads):
            pair = n * heads + h
            kc, vc = slice(h * dk, (h + 1) * dk), slice(h * dv, (h + 1) * dv)
            key, q, v = keys[rows, kc], query[rows, kc], values[rows, vc]
            spread, strict, late, a = block_masks(seg_col, seg_row, cum, cum_t, n, h)
            b = beta[rows, heads + h : heads + h + 1]
            inv = inv_ref[pair]
            delta = delta_ref[rows, vc]
            state = state_ref[pair]
            d_out = d_mixed[rows, vc]
            d_next = d_carry[h]
            key_late = key * late
            gram = dot(key, key, NT)
            score = dot(q, key, NT)
            d_score = dot(d_out, delta, NT)
            d_delta = dot(score * spread, d_out, TN)
            if not last:
                d_delta = d_delta + dot(key_late, d_next)
            d_right = dot(inv, d_delta, TN)
            d_lower = -dot(d_right, delta, NT) * strict
            d_value[rows, vc] = b * d_right
            dk_sum = jnp.zeros((GROUP, dk), F32)
            dq_sum = jnp.zeros((GROUP, dk), F32)
            d_b = jnp.sum(d_right * v, axis=-1, keepdims=True)
            d_c = jnp.zeros((GROUP, 1), F32)
            if n > 0:
                d_from = (-b * a) * d_right
                from_state = dot(key, state)
                d_b = d_b - a * jnp.sum(d_right * from_state, axis=-1, keepdims=True)
                dk_sum = dk_sum + dot(d_from, state, NT)
                reads = dot(d_out, state, NT)
                dq_sum = dq_sum + a * reads
                d_a = jnp.sum(q * reads, axis=-1, keepdims=True) - b * jnp.sum(
                    d_right * from_state, axis=-1, keepdims=True
                )
                d_state = dot(q * a, d_out, TN) + dot(key, d_from, TN)
                if not last:
                    a_last = a[GROUP - 1 : GROUP]
                    d_state = d_state + a_last * d_next
                    d_a = d_a + jnp.where(
                        row_col == GROUP - 1,
                        jnp.sum(jnp.sum(state * d_next, axis=-1, keepdims=True), axis=0, keepdims=True),
                        0.0,
                    )
                d_carry[h] = d_state
                d_c = d_c + d_a * a
            if not last:
                d_late_key = dot(delta, d_next, NT)
                dk_sum = dk_sum + late * d_late_key
                d_late = late * jnp.sum(key * d_late_key, axis=-1, keepdims=True)
                d_c = d_c - d_late + jnp.where(
                    row_col == GROUP - 1, jnp.sum(d_late, axis=0, keepdims=True), 0.0
                )
            d_pair = d_score * spread
            dq_sum = dq_sum + dot(d_pair, key)
            dk_sum = dk_sum + dot(d_pair, q, TN)
            gram_spread = gram * spread
            d_b = d_b + jnp.sum(d_lower * gram_spread, axis=-1, keepdims=True)
            d_gram = d_lower * (b * spread)
            dk_sum = dk_sum + dot(d_gram, key) + dot(d_gram, key, TN)
            cross = d_pair * score + d_gram * gram
            d_c = d_c + jnp.sum(cross, axis=-1, keepdims=True)
            falls = jnp.sum(cross, axis=0, keepdims=True)
            d_c = d_c - jnp.sum(eye * falls, axis=-1, keepdims=True)
            d_key[rows, kc] = dk_sum
            d_query[rows, kc] = dq_sum
            dc_block = dc_block + jnp.where(lane == h, d_c, 0.0)
            db_block = db_block + jnp.where(lane == heads + h, d_b, 0.0)
        d_cum[rows, :] = dc_block
        d_beta[rows, :] = db_block

    tick(2)
    d_log = block_cumsum_back(d_cum[...])
    grate_ref[...] = jnp.sum(d_log * -soft, axis=0, keepdims=True)
    sig = beta
    d_ref[:, b_base : b_base + LANES] = (
        d_log * -rate_row * sig + d_beta[...] * sig * (1.0 - sig)
    ).astype(BF16)

    for h in range(heads):
        kc, vc = slice(h * dk, (h + 1) * dk), slice(h * dv, (h + 1) * dv)
        for ref, taps, g_ref, d_unit, base, factor in (
            (q_ref, tq_ref, gq_ref, d_query, 0, scale),
            (k_ref, tk_ref, gk_ref, d_key, heads * dk, 1.0),
        ):
            proj = ref[:, kc]
            pre = conv(proj, taps[:, kc], keeps)
            act = jax.nn.silu(pre)
            normed, rate = unit(act)
            up = d_unit[:, kc] * factor
            d_act = rate * (up - normed * jnp.sum(up * normed, axis=-1, keepdims=True))
            d_proj, d_taps = conv_back(proj, taps[:, kc], keeps, d_act * silu_back(pre))
            d_ref[:, base + h * dk : base + (h + 1) * dk] = d_proj.astype(BF16)
            g_ref[:, kc] = d_taps
        proj = v_ref[:, vc]
        pre = conv(proj, tv_ref[:, vc], keeps)
        d_proj, d_taps = conv_back(proj, tv_ref[:, vc], keeps, d_value[:, vc] * silu_back(pre))
        d_ref[:, v_base + h * dv : v_base + (h + 1) * dv] = d_proj.astype(BF16)
        gv_ref[:, vc] = d_taps


def rows_of(index, count):
    return pl.ds(pl.multiple_of(index * count, count), count)


def enter(targets):
    barrier = pltpu.get_barrier_semaphore()
    for target in targets:
        pl.semaphore_signal(barrier, inc=1, device_id=target, device_id_type=MESH)
    pl.semaphore_wait(barrier, len(targets))


def order_of(n):
    steps = []
    for k in range(1, n // 2 + 1):
        steps.append(k)
        if n - k != k:
            steps.append(n - k)
    return steps


class Ring:
    def __init__(self, n):
        self.n = n
        self.me = lax.axis_index("tensor")
        self.steps = order_of(n)

    def to(self, k):
        return lax.rem(self.me + k, self.n)

    def source(self, k):
        return lax.rem(self.me + self.n - k, self.n)

    def targets(self):
        return [{"tensor": self.to(k)} for k in self.steps]

    def copy(self, k, src, dst, send, recv):
        return pltpu.make_async_remote_copy(
            src_ref=src, dst_ref=dst, send_sem=send.at[k - 1], recv_sem=recv.at[k - 1],
            device_id={"tensor": self.to(k)}, device_id_type=MESH,
        )

    def share(self, ref, send, recv):
        copies = {}
        for k in self.steps:
            copies[k] = self.copy(k, ref.at[self.me], ref.at[self.me], send, recv)
            copies[k].start()
        return copies


def pick(index, values):
    out = values[0]
    for i in range(1, len(values)):
        out = jnp.where(index == i, values[i], out)
    return out


class Line:
    def __init__(self, n):
        self.n, self.p = n, lax.axis_index("tensor")

    def has(self, side):
        return self.p != jnp.where(side == 0, self.n - 1, 0)

    def fed(self, side):
        return self.has(1 - side)

    def peer(self, side):
        return {"tensor": self.p + 1 - 2 * side}

    def place(self, i, key):
        n = self.n
        table = [sorted(range(n), key=lambda d: (d != p, key(p, d))) for p in range(n)]
        return pick(self.p, [row[i] for row in table])

    def arrival(self, i):
        return self.place(i, lambda p, d: (abs(d - p), d))

    def early(self, i):
        last = self.n - 1
        return self.place(i, lambda p, d: (last - d) + p if d > p else d + (last - p))

    def late(self, i):
        last = self.n - 1
        return self.place(i, lambda p, d: d + p if d > p else (last - d) + (last - p))

    def toward(self, d):
        return jnp.where(d > self.p, 0, 1), jnp.abs(d - self.p) - 1


PARTS = 2


def part_rows(count):
    step = count // PARTS
    return [pl.ds(c * step, step) for c in range(PARTS)]


class Gather:
    def __init__(self, line, ref, sems):
        self.line, self.ref, self.sems = line, ref, sems
        self.rows = part_rows(ref.shape[1])

    def copy(self, side, block, hop, c, peer):
        view = self.ref.at[block, self.rows[c]]
        return pltpu.make_async_remote_copy(
            src_ref=view, dst_ref=view,
            send_sem=self.sems.at[0, side, hop, c], recv_sem=self.sems.at[1, side, hop, c],
            device_id=self.line.peer(peer), device_id_type=MESH,
        )

    def start(self):
        for side in range(2):
            @pl.when(self.line.has(side))
            def _():
                for c in range(PARTS):
                    self.copy(side, self.line.p, 0, c, side).start()

    def arrive(self, block):
        side, hop = self.line.toward(block)
        side = 1 - side
        for c in range(PARTS):
            self.copy(side, block, hop, c, 1 - side).wait_recv()

            @pl.when(self.line.has(side))
            def _():
                self.copy(side, block, hop + 1, c, side).start()

    def hops(self, i):
        return jnp.abs(self.line.arrival(i) - self.line.p)

    def arrive_at(self, i):
        fresh = True if i == 1 else self.hops(i) != self.hops(i - 1)

        @pl.when(fresh)
        def _():
            self.arrive(self.line.arrival(i))

        if i + 1 < self.line.n:
            @pl.when(self.hops(i) == self.hops(i + 1))
            def _():
                self.arrive(self.line.arrival(i + 1))

    def done(self):
        for i in range(self.line.n):
            block = self.line.arrival(i)
            if i == 0:
                for side in range(2):
                    @pl.when(self.line.has(side))
                    def _():
                        for c in range(PARTS):
                            self.copy(side, block, 0, c, side).wait_send()
            else:
                side, hop = self.line.toward(block)
                side = 1 - side

                @pl.when(self.line.has(side))
                def _():
                    for c in range(PARTS):
                        self.copy(side, block, hop + 1, c, side).wait_send()


class Reduce:
    def __init__(self, line, held, out, box, sems):
        self.line, self.held, self.out, self.box, self.sems = line, held, out, box, sems
        self.rows = part_rows(out.shape[2])

    def copy(self, side, slot, c, peer):
        return pltpu.make_async_remote_copy(
            src_ref=self.out.at[side, slot, self.rows[c]],
            dst_ref=self.box.at[side, slot, self.rows[c]],
            send_sem=self.sems.at[0, side, slot, c], recv_sem=self.sems.at[1, side, slot, c],
            device_id=self.line.peer(peer), device_id_type=MESH,
        )

    def free(self, d):
        return jnp.logical_not(self.line.fed(self.line.toward(d)[0]))

    def emit(self, d):
        side, slot = self.line.toward(d)
        for c in range(PARTS):
            rows = self.rows[c]

            @pl.when(self.line.fed(side))
            def _():
                self.copy(side, slot + 1, c, 1 - side).wait_recv()
                self.held[d, rows] = self.held[d, rows] + self.box[side, slot + 1, rows].astype(F32)

            self.out[side, slot, rows] = self.held[d, rows].astype(BF16)
            self.copy(side, slot, c, side).start()

    def finish(self):
        for side in range(2):
            @pl.when(self.line.fed(side))
            def _():
                for c in range(PARTS):
                    self.copy(side, 0, c, 1 - side).wait_recv()
                self.held[self.line.p] = self.held[self.line.p] + self.box[side, 0].astype(F32)

    def done(self):
        for i in range(1, self.line.n):
            side, slot = self.line.toward(self.line.early(i))
            for c in range(PARTS):
                self.copy(side, slot, c, side).wait_send()


def fill(target, column, bits, lhs, values):
    width = lhs.shape[1]
    rows = width >> bits
    step = max(rows, 256)
    for base in range(0, width, step):
        value = dot(lhs[:, base : base + step], values, TN).astype(BF16)
        for inner in range(0, step, rows):
            block = (base + inner) // rows
            lead = tuple((block >> b) % 2 for b in range(bits - 1, -1, -1))
            target[lead + (slice(None), slice(column, column + values.shape[1]))] = value[
                inner : inner + rows
            ]


class Scatter:
    def __init__(self, bits, source, result, inbox, total, streams, sems):
        self.bits, self.source, self.result = bits, source, result
        self.inbox, self.total, self.streams, self.sems = inbox, total, streams, sems
        self.dp = lax.axis_index("dp")
        self.copies = []

    def bit(self, b):
        return lax.rem(self.dp // (1 << b), 2)

    def partner(self, b):
        return {"dp": self.dp + (1 - 2 * self.bit(b)) * (1 << b)}

    def targets(self):
        return [self.partner(b) for b in range(self.bits)]

    def send(self, b, src, dst, slot):
        copy = pltpu.make_async_remote_copy(
            src_ref=src, dst_ref=dst, send_sem=self.sems.at[0, slot], recv_sem=self.sems.at[1, slot],
            device_id=self.partner(b), device_id_type=MESH,
        )
        copy.start()
        self.copies.append(copy)
        return copy

    def orders(self):
        rest = list(range(1, self.bits))
        return rest, rest[::-1]

    def step(self, phase):
        if phase == 0:
            lead = (slice(None),) * (self.bits - 1)
            self.waiting = [self.send(0, self.source.at[lead + (1 - self.bit(0),)], self.inbox, 0)]
            return
        if phase == 1:
            lead = (slice(None),) * (self.bits - 1)
            self.waiting[0].wait_recv()
            self.total[...] = (
                self.source[lead + (self.bit(0),)].astype(F32) + self.inbox[...].astype(F32)
            ).astype(BF16)
            self.held = [(self.total, list(range(self.bits - 1, 0, -1)))] * 2
        waiting = []
        for s, order in enumerate(self.orders()):
            low, high, sums, boxes = self.streams[s]
            if phase > 1:
                b = order[phase - 2]
                ref, axes = self.held[s]
                self.waiting[s].wait_recv()
                columns = (slice(None), slice(low, high) if phase == 2 else slice(None))
                lead = tuple(self.bit(b) if a == b else slice(None) for a in axes)
                value = ref[lead + columns].astype(F32) + boxes[phase - 2][...].astype(F32)
                if phase == self.bits:
                    self.result[:, low:high] = value
                else:
                    sums[phase - 2][...] = value.astype(BF16)
                    self.held[s] = (sums[phase - 2], [a for a in axes if a != b])
            if phase < self.bits:
                b = order[phase - 1]
                ref, axes = self.held[s]
                columns = (slice(None), slice(low, high) if phase == 1 else slice(None))
                lead = tuple(1 - self.bit(b) if a == b else slice(None) for a in axes)
                slot = 1 + s * (self.bits - 1) + phase - 1
                waiting.append(self.send(b, ref.at[lead + columns], boxes[phase - 1], slot))
        self.waiting = waiting

    def finish(self):
        for copy in self.copies:
            copy.wait_send()


def scatter_scratch(bits, rows, width):
    middle = width // (2 * LANES) * LANES
    shapes = [
        pltpu.VMEM((rows, width), F32),
        pltpu.VMEM((2,) * (bits - 1) + (rows, width), BF16),
        pltpu.VMEM((2,) * (bits - 1) + (rows, width), BF16),
    ]
    for low, high in ((0, middle), (middle, width)):
        for kind in range(2):
            for left in range(bits - 2, -1, -1):
                shapes.append(pltpu.VMEM((2,) * left + (rows, high - low), BF16))
    shapes.append(pltpu.SemaphoreType.DMA((2, 2 * bits - 1)))
    return shapes


def scatter_of(bits, source, scratch):
    result, inbox, total = scratch[:3]
    width = result.shape[1]
    middle = width // (2 * LANES) * LANES
    each = bits - 1
    refs = scratch[3:-1]
    streams = []
    for s, (low, high) in enumerate(((0, middle), (middle, width))):
        part = refs[2 * each * s : 2 * each * (s + 1)]
        streams.append((low, high, part[:each], part[each:]))
    return Scatter(bits, source, result, inbox, total, streams, scratch[-1])


def narrow_parts(wd_ref, wb_ref, heads, wdb_ref):
    wdb_ref[...] = jnp.zeros_like(wdb_ref)
    wdb_ref[0:heads, :] = wd_ref[...].astype(F32)
    wdb_ref[heads : 2 * heads, :] = wb_ref[...].astype(F32)


def project_kernel(
    n, heads, dk, dv,
    x_ref, grad_ref, gain_ref, wq_ref, wk_ref, wv_ref, wg_ref, wd_ref, wb_ref, *rest
):
    consts = rest[:6]
    xn_ref, gfull_ref, q_ref, k_ref, v_ref, gate_ref, db_ref = rest[6:13]
    outs = rest[13:18]
    scratch = rest[18:22]
    xsems, gsems, wdb_ref, rate_ref = rest[22:]
    narrow_parts(wd_ref, wb_ref, heads, wdb_ref)
    rate_ref[...] = jnp.zeros_like(rate_ref)
    rate_ref[:, :heads] = consts[4][...]
    consts = consts[:4] + (rate_ref,) + consts[5:]
    ring = Ring(n)
    count = x_ref.shape[0]
    x = x_ref[...].astype(F32)
    rate = lax.rsqrt(jnp.mean(x * x, axis=-1, keepdims=True) + EPS_NORM)
    xn_ref[ring.me] = (x * rate * gain_ref[...]).astype(BF16)
    gfull_ref[ring.me] = grad_ref[...]
    enter(ring.targets())
    line = Line(n)
    gather = Gather(line, xn_ref, xsems)
    share = Gather(line, gfull_ref, gsems)
    gather.start()

    def project(index):
        rows = rows_of(index, count)
        chunk = xn_ref[index]
        for w, out in ((wq_ref, q_ref), (wk_ref, k_ref), (wv_ref, v_ref), (wg_ref, gate_ref)):
            out[rows, :] = dot(chunk, w[...])
        db_ref[rows, :] = dot(chunk, wdb_ref[...], NT)

    project(line.p)
    for i in range(1, n):
        gather.arrive_at(i)
        if i == n - 1:
            share.start()
        project(line.arrival(i))

    mixer_forward_kernel(
        heads, dk, dv, q_ref, k_ref, v_ref, gate_ref, db_ref, *consts, *outs, *scratch,
        tick=lambda i: share.arrive_at(i) if i < n else None,
    )
    for i in range(3, n):
        share.arrive_at(i)
    gather.done()
    share.done()


def project_mix(n, heads, x, grad, gain, wq, wk, wv, wg, wd, wb, *consts):
    count, width = x.shape
    length = count * n
    dk, dv = wq.shape[1] // heads, wv.shape[1] // heads
    pairs = heads * (length // GROUP)
    f32 = lambda *shape: jax.ShapeDtypeStruct(shape, F32)
    shapes = (
        jax.ShapeDtypeStruct((n, count, width), BF16),
        jax.ShapeDtypeStruct((n, count, width), BF16),
        f32(length, heads * dk), f32(length, heads * dk), f32(length, heads * dv),
        f32(length, heads * dv), f32(length, LANES),
        jax.ShapeDtypeStruct((length, heads * dv), BF16),
        f32(pairs, GROUP, GROUP), f32(length, heads * dv), f32(pairs, dk, dv),
        f32(length, heads * dv),
    )
    dma = pltpu.SemaphoreType.DMA((2, 2, n - 1, PARTS))
    return pl.pallas_call(
        partial(project_kernel, n, heads, dk, dv),
        out_shape=shapes,
        in_specs=vmem_specs(15),
        out_specs=tuple(vmem_specs(12)),
        scratch_shapes=[
            pltpu.VMEM((length, heads * dk), F32), pltpu.VMEM((length, heads * dk), F32),
            pltpu.VMEM((length, heads * dv), F32), pltpu.VMEM((heads, dk, dv), F32),
            dma, dma, pltpu.VMEM((LANES, width), F32), pltpu.VMEM((1, LANES), F32),
        ],
        compiler_params=pltpu.CompilerParams(
            collective_id=0, has_side_effects=True, vmem_limit_bytes=PROJECT_BYTES
        ),
        name="project_mix",
    )(x, grad, gain, wq, wk, wv, wg, wd, wb, *consts)


def middle_kernel(
    n, bits,
    gated_ref, x_ref, grad_ref, gfull_ref, wout_ref, gain_ref, wfg_ref, wfu_ref, wfd_ref,
    resid_ref, dresid_ref, ffn_ref, dgated_ref, gout_ref, first_ref, gfgain_ref,
    out_send, out_box, hn, dh_send, dh_box, dres, d_act, act, d_in, d_val, held, grads, sems,
    *scratch
):
    ring = Ring(n)
    count, width = x_ref.shape
    columns = wfg_ref.shape[0]
    padded = columns + (-columns % LANES)
    enter(ring.targets() + scatter_of(bits, grads, scratch).targets())
    flat = lambda ref: ref[...].reshape(n * count, ref.shape[2])
    if padded > columns:
        for i in range(3):
            tail = slice((i + 1) * padded - LANES, (i + 1) * padded)
            grads[(slice(None),) * (bits + 1) + (tail,)] = jnp.zeros(
                grads.shape[:-1] + (LANES,), BF16
            )

    def feed(index):
        chunk = hn[index]
        up_in = dot(chunk, wfg_ref[...], NT)
        up_val = dot(chunk, wfu_ref[...], NT)
        sig = sigmoid(up_in)
        d_chunk = d_act[index]
        half = up_in * sig
        act[index] = (half * up_val).astype(BF16)
        d_in[index] = (d_chunk * up_val * sig * (1.0 + up_in * (1.0 - sig))).astype(BF16)
        d_val[index] = (d_chunk * half).astype(BF16)
        held[index] = dot(d_in[index], wfg_ref[...]) + dot(d_val[index], wfu_ref[...])

    line = Line(n)
    p = line.p
    scatter = scatter_of(bits, grads, scratch)
    part = lambda d: dot(gated_ref[rows_of(d, count), :], wout_ref[...])
    sums = Reduce(line, held, out_send, out_box, sems.at[0])
    for i in range(1, n):
        d = line.early(i)
        held[d] = part(d)
        sums.emit(d)
    held[p] = x_ref[...].astype(F32) + part(p)
    for i in range(n):
        d_act[i] = dot(gfull_ref[i], wfd_ref[...], NT)
    sums.finish()
    resid = held[p]
    resid_ref[...] = resid
    rate = lax.rsqrt(jnp.mean(resid * resid, axis=-1, keepdims=True) + EPS_NORM)
    hn[p] = (resid * rate * gain_ref[...]).astype(BF16)
    share = Gather(line, hn, sems.at[1])
    share.start()
    feed(p)
    back = Reduce(line, held, dh_send, dh_box, sems.at[2])
    for i in range(1, n):
        share.arrive_at(i)
        d = line.arrival(i)
        feed(d)
        pl.when(back.free(d))(partial(back.emit, d))
    for i in range(1, n):
        d = line.late(i)
        pl.when(jnp.logical_not(back.free(d)))(partial(back.emit, d))
    for i, (left, right) in enumerate(((hn, d_in), (hn, d_val), (gfull_ref, act))):
        fill(grads, i * padded, bits, flat(left), flat(right))
    scatter.step(0)
    back.finish()
    d_hnorm = held[p]
    resid = resid_ref[...]
    rate = lax.rsqrt(jnp.mean(resid * resid, axis=-1, keepdims=True) + EPS_NORM)
    plain = resid * rate
    gfgain_ref[...] = jnp.sum(d_hnorm * plain, axis=0, keepdims=True)
    up = d_hnorm * gain_ref[...]
    d_resid = grad_ref[...].astype(F32) + rate * (
        up - plain * jnp.mean(up * plain, axis=-1, keepdims=True)
    )
    dresid_ref[...] = d_resid
    dres[p] = d_resid.astype(BF16)
    spread = Gather(line, dres, sems.at[3])
    spread.start()

    def back_out(d):
        dgated_ref[rows_of(d, count), :] = dot(dres[d], wout_ref[...], NT)

    back_out(p)
    scatter.step(1)
    for i in range(1, n):
        spread.arrive_at(i)
        back_out(line.arrival(i))
        if i == 1:
            for k in range(n):
                ffn_ref[k * count : (k + 1) * count, :] = dot(act[k], wfd_ref[...]).astype(BF16)
        if i == n - 1:
            scatter.step(2)
    lhs = flat(dres)
    step = math.gcd(width, 256)
    for base in range(0, width, step):
        gout_ref[base : base + step, :] = dot(
            lhs[:, base : base + step], gated_ref[...], TN
        ).astype(BF16)
    for phase in range(3, bits + 1):
        scatter.step(phase)
    first_ref[...] = scratch[0][...]
    for group in (sums, share, back, spread):
        group.done()
    scatter.finish()


def middle(n, bits, gated, x, grad, gfull, wout, gain, wfg, wfu, wfd):
    count, width = x.shape
    length = n * count
    inner, columns = wout.shape[0], wfg.shape[0]
    padded = columns + (-columns % LANES)
    rows = width >> bits
    f32 = lambda *shape: jax.ShapeDtypeStruct(shape, F32)
    slots = pltpu.VMEM((2, n - 1, count, width), BF16)
    return pl.pallas_call(
        partial(middle_kernel, n, bits),
        out_shape=(
            f32(count, width), f32(count, width),
            jax.ShapeDtypeStruct((length, width), BF16),
            f32(length, inner),
            jax.ShapeDtypeStruct((width, inner), BF16),
            f32(rows, 3 * padded),
            f32(1, width),
        ),
        in_specs=vmem_specs(9),
        out_specs=tuple(vmem_specs(7)),
        scratch_shapes=[
            slots, slots, pltpu.VMEM((n, count, width), BF16), slots, slots,
            pltpu.VMEM((n, count, width), BF16),
            pltpu.VMEM((n, count, columns), F32),
            pltpu.VMEM((n, count, columns), BF16),
            pltpu.VMEM((n, count, columns), BF16),
            pltpu.VMEM((n, count, columns), BF16),
            pltpu.VMEM((n, count, width), F32),
            pltpu.VMEM((2,) * bits + (rows, 3 * padded), BF16),
            pltpu.SemaphoreType.DMA((4, 2, 2, n - 1, PARTS)),
        ] + scatter_scratch(bits, rows, 3 * padded),
        compiler_params=pltpu.CompilerParams(
            collective_id=1, has_side_effects=True, vmem_limit_bytes=MIDDLE_BYTES
        ),
        name="middle",
    )(gated, x, grad, gfull, wout, gain, wfg, wfu, wfd)


def back_kernel(n, bits, heads, dk, dv, *refs):
    mixer_in, (gout_ref, xn_ref, ffn_ref, resid_ref) = refs[:16], refs[16:20]
    mixer_out, (block_ref, first_ref) = refs[20:26], refs[26:28]
    mixer_scratch, (boxes, fsems, rate_ref, grads), scratch = refs[28:38], refs[38:42], refs[42:]
    rate_ref[...] = jnp.zeros_like(rate_ref)
    rate_ref[:, :heads] = mixer_in[9][...]
    mixer_in = mixer_in[:9] + (rate_ref,) + mixer_in[10:]
    d_ref = mixer_out[0]
    ring = Ring(n)
    scatter = scatter_of(bits, grads, scratch)
    enter(ring.targets() + scatter.targets())
    inner = gout_ref.shape[1]
    rows = gout_ref.shape[0] >> bits

    def tick(phase):
        if phase == 0:
            for block in range(1 << bits):
                lead = tuple((block >> b) % 2 for b in range(bits - 1, -1, -1))
                grads[lead + (slice(None), slice(0, inner))] = gout_ref[
                    block * rows : (block + 1) * rows
                ]
            lhs = xn_ref[...].reshape(d_ref.shape[0], xn_ref.shape[2])
            base = 2 * heads * (dk + dv) - heads * dv
            fill(grads, inner, bits, lhs, d_ref[:, base : base + heads * dv])
        scatter.step(phase)

    count = resid_ref.shape[0]
    sends = {}
    for k in ring.steps:
        sends[k] = ring.copy(
            k, ffn_ref.at[rows_of(ring.to(k), count), :], boxes.at[k - 1], fsems.at[0], fsems.at[1]
        )
        sends[k].start()
    mixer_backward_kernel(heads, dk, dv, *mixer_in, *mixer_out, *mixer_scratch, tick=tick)
    for phase in range(3, bits + 1):
        scatter.step(phase)
    block = resid_ref[...] + ffn_ref[rows_of(ring.me, count), :].astype(F32)
    for k in ring.steps:
        sends[k].wait_recv()
        block = block + boxes[k - 1].astype(F32)
    block_ref[...] = block.astype(BF16)
    first_ref[...] = scratch[0][...]
    for k in ring.steps:
        sends[k].wait_send()
    scatter.finish()


def backward(n, bits, heads, mixer_in, g_out, xnorm, ffn, resid):
    q, v = mixer_in[0], mixer_in[2]
    length = q.shape[0]
    dk, dv = q.shape[1] // heads, v.shape[1] // heads
    wide_out = 2 * heads * dk + 2 * heads * dv + LANES
    count, width = resid.shape
    rows = width >> bits
    second = g_out.shape[1] + heads * dv
    f32 = lambda *shape: jax.ShapeDtypeStruct(shape, F32)
    shapes = (
        jax.ShapeDtypeStruct((length, wide_out), BF16),
        f32(*mixer_in[6].shape), f32(*mixer_in[7].shape), f32(*mixer_in[8].shape),
        f32(1, LANES), f32(1, dv),
        jax.ShapeDtypeStruct((count, width), BF16),
        f32(rows, second),
    )
    narrow, broad = (length, heads * dk), (length, heads * dv)
    return pl.pallas_call(
        partial(back_kernel, n, bits, heads, dk, dv),
        out_shape=shapes,
        in_specs=vmem_specs(20),
        out_specs=tuple(vmem_specs(8)),
        scratch_shapes=[
            pltpu.VMEM(narrow, F32), pltpu.VMEM(narrow, F32), pltpu.VMEM(broad, F32),
            pltpu.VMEM(broad, F32), pltpu.VMEM(narrow, F32), pltpu.VMEM(narrow, F32),
            pltpu.VMEM(broad, F32), pltpu.VMEM((heads, dk, dv), F32),
            pltpu.VMEM((length, LANES), F32), pltpu.VMEM((length, LANES), F32),
            pltpu.VMEM((n - 1, count, width), BF16), pltpu.SemaphoreType.DMA((2, n - 1)),
            pltpu.VMEM((1, LANES), F32),
            pltpu.VMEM((2,) * bits + (rows, second), BF16),
        ] + scatter_scratch(bits, rows, second),
        compiler_params=pltpu.CompilerParams(
            collective_id=2, has_side_effects=True, vmem_limit_bytes=BACK_BYTES
        ),
        name="mixer_back",
    )(*mixer_in, g_out, xnorm, ffn, resid)


def last_kernel(n, bits, heads, dk, dv, *refs):
    (d_ref, xn_ref, x_ref, gain_ref, dresid_ref, wq_ref, wk_ref, wv_ref, wg_ref, wd_ref, wb_ref,
     gq_ref, gk_ref, gv_ref, grate_ref, gogain_ref, gfgain_ref) = refs[:17]
    dx_ref, rest_ref, final_ref = refs[17:20]
    grads, dx_send, dx_box, gains, small, small_in, sems, dx_sems, small_sems, wdb_ref, held = (
        refs[20:31]
    )
    scratch = refs[31:]
    narrow_parts(wd_ref, wb_ref, heads, wdb_ref)
    ring = Ring(n)
    scatter = scatter_of(bits, grads, scratch)
    enter(ring.targets() + scatter.targets())
    count, width = x_ref.shape
    weights = (wq_ref, wk_ref, wv_ref, wg_ref)
    span = gains.shape[2]
    line = Line(n)
    p = line.p
    sums = Reduce(line, held, dx_send, dx_box, dx_sems)
    g_again = jnp.zeros((1, width), F32)
    for i in list(range(1, n)) + [0]:
        d = line.early(i)
        rows = rows_of(d, count)
        base, total = 0, None
        for w in weights:
            part = dot(d_ref[rows, base : base + w.shape[1]], w[...], NT)
            total = part if total is None else total + part
            base += w.shape[1]
        total = total + dot(d_ref[rows, base:], wdb_ref[...])
        held[d] = total
        g_again = g_again + jnp.sum(total * xn_ref[d].astype(F32), axis=0, keepdims=True)
        if i > 0:
            pl.when(sums.free(d))(partial(sums.emit, d))
    small[0] = jnp.zeros(small.shape[1:], F32)
    narrow, broad = heads * dk, heads * dv
    taps = gq_ref.shape[0]
    small[0, 0:taps, :narrow] = gq_ref[...]
    small[0, 0:taps, narrow : 2 * narrow] = gk_ref[...]
    small[0, 0:taps, 2 * narrow : 2 * narrow + broad] = gv_ref[...]
    small[0, 8:9, :LANES] = grate_ref[...]
    small[0, 16:17, :width] = g_again / gain_ref[...]
    small[0, 17:18, :width] = gfgain_ref[...]
    small[0, 18:19, :dv] = gogain_ref[...]
    swaps = []

    def swap(b):
        copy = pltpu.make_async_remote_copy(
            src_ref=small.at[b], dst_ref=small_in.at[b],
            send_sem=small_sems.at[0, b], recv_sem=small_sems.at[1, b],
            device_id=scatter.partner(b), device_id_type=MESH,
        )
        copy.start()
        swaps.append(copy)

    def swapped(b):
        swaps[b].wait_recv()
        small[b + 1] = small[b] + small_in[b]

    def pass_on(i):
        d = line.early(i)
        pl.when(jnp.logical_not(sums.free(d)))(partial(sums.emit, d))

    swap(0)
    lhs = xn_ref[...].reshape(n * count, width)
    front = 2 * narrow + broad
    fill(grads, front, bits, lhs, d_ref[:, front + broad :])
    swapped(0)
    if bits > 1:
        swap(1)
    fill(grads, 0, bits, lhs, d_ref[:, :front])
    scatter.step(0)
    for b in range(1, bits):
        swapped(b)
        if b + 1 < bits:
            swap(b + 1)
        if b == 1:
            pass_on(1)
    scatter.step(1)
    gains[p] = small[bits, 16:24, :]
    shares = ring.share(gains, sems.at[0], sems.at[1])
    for i in range(1 if bits < 2 else 2, n):
        pass_on(i)
    for phase in range(2, bits):
        scatter.step(phase)
    sums.finish()
    d_xnorm = held[p]
    x = x_ref[...].astype(F32)
    rate = lax.rsqrt(jnp.mean(x * x, axis=-1, keepdims=True) + EPS_NORM)
    plain = x * rate
    up = d_xnorm * gain_ref[...]
    dx_ref[...] = (
        dresid_ref[...] + rate * (up - plain * jnp.mean(up * plain, axis=-1, keepdims=True))
    ).astype(BF16)
    for phase in range(max(bits, 2), bits + 1):
        scatter.step(phase)
    rest_ref[...] = scratch[0][...]
    for k in ring.steps:
        shares[k].wait_recv()
    total = gains[0]
    for i in range(1, n):
        total = total + gains[i]
    final_ref[...] = small[bits]
    final_ref[16:24, :] = total
    sums.done()
    for k in ring.steps:
        shares[k].wait_send()
    for copy in swaps:
        copy.wait_send()
    scatter.finish()


def last(n, bits, heads, *args):
    d_cat, xn, x, _, _, wq, _, wv = args[:8]
    narrow, broad = wq.shape[1], wv.shape[1]
    dk, dv = narrow // heads, broad // heads
    count, width = x.shape
    rows = width >> bits
    span = max(width, 2 * narrow + broad)
    f32 = lambda *shape: jax.ShapeDtypeStruct(shape, F32)
    slots = pltpu.VMEM((2, n - 1, count, width), BF16)
    cut = d_cat.shape[1] - broad
    return pl.pallas_call(
        partial(last_kernel, n, bits, heads, dk, dv),
        out_shape=(
            jax.ShapeDtypeStruct((count, width), BF16),
            f32(rows, cut), f32(24, span),
        ),
        in_specs=vmem_specs(17),
        out_specs=tuple(vmem_specs(3)),
        scratch_shapes=[
            pltpu.VMEM((2,) * bits + (rows, cut), BF16),
            slots, slots,
            pltpu.VMEM((n, 8, span), F32),
            pltpu.VMEM((bits + 1, 24, span), F32),
            pltpu.VMEM((bits, 24, span), F32),
            pltpu.SemaphoreType.DMA((2, n - 1)),
            pltpu.SemaphoreType.DMA((2, 2, n - 1, PARTS)),
            pltpu.SemaphoreType.DMA((2, bits)),
            pltpu.VMEM((LANES, width), F32),
            pltpu.VMEM((n, count, width), F32),
        ] + scatter_scratch(bits, rows, cut),
        compiler_params=pltpu.CompilerParams(
            collective_id=3, has_side_effects=True, vmem_limit_bytes=LAST_BYTES
        ),
        name="last",
    )(*args)


def finish_kernel(heads, dk, dv, columns, taps, *refs):
    block_in, dx_in, first, second, rest, small = refs[:6]
    (block, dx, again, sq, sk, sv, sg, sd, sb, cq, ck, cv, rate, ogain, sout, fgain,
     sgate, sup, sdown) = refs[6:]
    block[...] = block_in[...]
    dx[...] = dx_in[...]
    narrow, broad = heads * dk, heads * dv
    width = again.shape[1]
    sq[...] = rest[:, :narrow]
    sk[...] = rest[:, narrow : 2 * narrow]
    base = 2 * narrow
    sv[...] = rest[:, base : base + broad]
    inner = sout.shape[0]
    sg[...] = second[:, inner:]
    tail = rest[:, base + broad :].T
    sd[...] = tail[0:heads]
    sb[...] = tail[heads : 2 * heads]
    cq[...] = small[0:taps, :narrow]
    ck[...] = small[0:taps, narrow : 2 * narrow]
    cv[...] = small[0:taps, 2 * narrow : 2 * narrow + broad]
    rate[...] = small[8:9, :heads]
    again[...] = small[16:17, :width]
    fgain[...] = small[17:18, :width]
    ogain[...] = small[18:19, :dv]
    padded = columns + (-columns % LANES)
    sgate[...] = first[:, :padded].T[:columns]
    sup[...] = first[:, padded : 2 * padded].T[:columns]
    sdown[...] = first[:, 2 * padded : 3 * padded].T[:columns]
    sout[...] = second[:, :inner].T


def finish(heads, dk, dv, columns, taps, block, dx, first, second, rest, small):
    rows, width = rest.shape[0], block.shape[1]
    narrow, broad = heads * dk, heads * dv
    inner = second.shape[1] - broad
    f32 = lambda *shape: jax.ShapeDtypeStruct(shape, F32)
    return pl.pallas_call(
        partial(finish_kernel, heads, dk, dv, columns, taps),
        out_shape=(
            jax.ShapeDtypeStruct(block.shape, BF16), jax.ShapeDtypeStruct(dx.shape, BF16),
            f32(1, width), f32(rows, narrow), f32(rows, narrow), f32(rows, broad),
            f32(rows, broad), f32(heads, rows), f32(heads, rows), f32(taps, narrow),
            f32(taps, narrow), f32(taps, broad), f32(1, heads), f32(1, dv), f32(inner, rows),
            f32(1, width), f32(columns, rows), f32(columns, rows), f32(columns, rows),
        ),
        in_specs=vmem_specs(6),
        out_specs=tuple(vmem_specs(19)),
        compiler_params=pltpu.CompilerParams(vmem_limit_bytes=24 << 20),
        name="finish",
    )(block, dx, first, second, rest, small)


def body(
    n,
    bits,
    tokens,
    seg_ids,
    attn_gain,
    w_query,
    w_key,
    w_value,
    w_gate,
    w_decay,
    w_beta,
    conv_query,
    conv_key,
    conv_value,
    decay_rate,
    out_gain,
    w_out,
    ffn_gain,
    w_ffn_gate,
    w_ffn_up,
    w_ffn_down,
    grad_out,
):
    heads = w_decay.shape[1]
    row = lambda array: array.reshape(1, -1)
    columns = w_ffn_gate.shape[1]
    taps = conv_query.shape[0]
    dk, dv = w_query.shape[1] // heads, w_value.shape[1] // heads
    consts = (seg_ids, conv_query, conv_key, conv_value, row(decay_rate), row(out_gain))
    xnorm, grad_full, *projs, gated, inv, delta, states, mixed = project_mix(
        n, heads, tokens, grad_out, row(attn_gain), w_query, w_key, w_value, w_gate,
        w_decay.T, w_beta.T, *consts
    )
    resid, d_resid, ffn, d_gated, g_out, first, g_fgain = middle(
        n, bits, gated, tokens, grad_out, grad_full, w_out, row(ffn_gain),
        w_ffn_gate.T, w_ffn_up.T, w_ffn_down
    )
    mixer_in = (*projs, *consts, inv, delta, states, mixed, d_gated)
    d_cat, g_cq, g_ck, g_cv, g_rate, g_ogain, block_out, second = backward(
        n, bits, heads, mixer_in, g_out, xnorm, ffn, resid
    )
    grad_tokens, rest, small = last(
        n, bits, heads, d_cat, xnorm, tokens, row(attn_gain), d_resid, w_query, w_key, w_value,
        w_gate, w_decay.T, w_beta.T, g_cq, g_ck, g_cv, g_rate, g_ogain, g_fgain
    )
    (block_out, grad_tokens, again, s_query, s_key, s_value, s_gate, s_decay, s_beta, cq, ck, cv,
     rate, ogain, s_out, fgain, s_fgate, s_fup, s_down) = finish(
        heads, dk, dv, columns, taps, block_out, grad_tokens, first, second, rest, small
    )
    flat = lambda array: array.reshape(-1)
    return (
        block_out, grad_tokens, flat(again), s_query, s_key, s_value, s_gate, s_decay.T, s_beta.T,
        cq, ck, cv, flat(rate), flat(ogain), s_out, flat(fgain), s_fgate.T, s_fup.T, s_down,
    )


def solution(mesh):
    in_specs = (
        P(("dp", "tensor"), None),
        P("dp", None),
        P(),
        P(None, "tensor"),
        P(None, "tensor"),
        P(None, "tensor"),
        P(None, "tensor"),
        P(None, "tensor"),
        P(None, "tensor"),
        P(None, "tensor"),
        P(None, "tensor"),
        P(None, "tensor"),
        P("tensor"),
        P(),
        P("tensor", None),
        P(),
        P(None, "tensor"),
        P(None, "tensor"),
        P("tensor", None),
        P(("dp", "tensor"), None),
    )
    out_specs = (
        P(("dp", "tensor"), None),
        P(("dp", "tensor"), None),
        P(),
        P("dp", "tensor"),
        P("dp", "tensor"),
        P("dp", "tensor"),
        P("dp", "tensor"),
        P("dp", "tensor"),
        P("dp", "tensor"),
        P(None, "tensor"),
        P(None, "tensor"),
        P(None, "tensor"),
        P("tensor"),
        P(),
        P("tensor", "dp"),
        P(),
        P("dp", "tensor"),
        P("dp", "tensor"),
        P("tensor", "dp"),
    )
    n = mesh.shape["tensor"]
    bits = mesh.shape["dp"].bit_length() - 1
    return jax.shard_map(partial(body, n, bits), mesh=mesh, in_specs=in_specs, out_specs=out_specs, check_vma=False)
```
